32 devices in a mesh: section: 4 (over x, core), group: 8 (over z, y).
Axes of the slice: x: 2, y: 2, z: 4, core: 2. Of those that a mesh axis runs over, the one named last changes fastest.
Arguments:
- acts: bfloat16 [4, 1024, 2048], P('section', 'group'), may hold values from -45 to 45
- start_basis: float32 [4, 2048, 768], P('section', 'group'), may hold values from -6 to 6
- out_proj: bfloat16 [4, 8192, 2048], P('section', 'group'), may hold values from -6 to 6
- in_proj: bfloat16 [4, 2048, 2048], P('section', None, 'group'), may hold values from -6 to 6
Outputs:
- rotated_out: bfloat16 [4, 8192, 768], P('section', 'group')
- rotated_in: bfloat16 [4, 768, 2048], P('section', None, 'group')
The draws below stay inside these ranges and needn't reach their ends.
All inputs are finite; a program needn't handle non-finite values.
Results may differ from the reference program's by a relative error of at most 0.0084.
Values may be sent and summed in bfloat16 or wider, within the bound.
No kernel may reach another device: no remote copies, remote signals or barrier semaphores. Data moves between devices by JAX's collectives and lax.ppermute only.
A program may use at most 64 MiB of HBM per device.

```python
import jax
import jax.numpy as jnp
from jax import lax

D = 2048
FF = 8192
FQ = 2048
DIRS = 768
ITERS = 1
TOKENS = 1024
N_SECTION = 4


def draw_acts(key, part):
    keys = jax.random.split(key, 3)
    shape = (N_SECTION, TOKENS, D)
    columns = jnp.exp(jax.random.uniform(keys[0], (N_SECTION, 1, D), jnp.float32) * jnp.log(10.0))
    place = jnp.arange(TOKENS, dtype=jnp.float32) / TOKENS
    scales = (1.0 + 2.0 * place)[None, :, None] * jnp.exp(jax.random.uniform(keys[1], (N_SECTION, TOKENS, 1), jnp.float32) * jnp.log(3.0))
    base = jnp.clip(jax.random.normal(keys[2], shape, jnp.float32), -5.0, 5.0)
    return (0.1 * base * scales * columns).astype(jnp.bfloat16)


def block_levels(own_key, shape, pieces, low, top_value):
    level, own = 1.0, jax.random.fold_in(own_key, 6)
    for dim, shards_of in pieces:
        heights = jnp.exp(jax.random.uniform(jax.random.fold_in(own, dim), (shards_of,), jnp.float32, low / len(pieces), top_value / len(pieces)))
        level = level * jnp.repeat(heights, shape[dim] // shards_of).reshape([-1 if axis == dim else 1 for axis in range(len(shape))])
    return level


def gaussian(stream_key, shape, spread, most, pieces=(), kind=jnp.bfloat16):
    array = spread * jax.random.normal(stream_key, shape, jnp.float32)
    if pieces:
        array = array * block_levels(stream_key, shape, pieces, -0.22, 0.18)
    return jnp.clip(array, -most, most).astype(kind)


def setup_inputs(seed: int = 0) -> dict:
    splits = jax.random.split(jax.random.key(seed), 5)
    return {
        "acts": draw_acts(jax.random.fold_in(splits[4], 71), 0),
        "start_basis": gaussian(splits[1], (N_SECTION, D, DIRS), 1.0, 6.0, ((0, 4), (1, 8)), jnp.float32),
        "out_proj": gaussian(splits[2], (N_SECTION, FF, D), 1.0, 6.0, ((0, 4), (1, 8))),
        "in_proj": gaussian(splits[3], (N_SECTION, D, FQ), 1.0, 6.0, ((0, 4), (2, 8))),
    }


def orthonormal(image):
    gram = jnp.dot(image.T.astype(jnp.float32), image.astype(jnp.float32), precision=lax.Precision.HIGHEST, preferred_element_type=jnp.float32)
    factor = jnp.linalg.cholesky(gram)
    return jax.scipy.linalg.solve_triangular(factor, image.T, lower=True).T

def leading(tokens, start):
    lowered = start.astype(jnp.bfloat16)
    for step in range(ITERS):
        projected = jnp.dot(tokens.astype(jnp.float32), lowered.astype(jnp.float32), preferred_element_type=jnp.float32).astype(jnp.bfloat16)
        image = lax.dot_general(tokens.astype(jnp.float32), projected.astype(jnp.float32), (((0,), (0,)), ((), ())), preferred_element_type=jnp.float32)
        lowered = orthonormal(image).astype(jnp.bfloat16)
    return lowered

def reference(acts, start_basis, out_proj, in_proj):
    finals = [leading(acts[section_id], start_basis[section_id]) for section_id in range(N_SECTION)]
    outs_list = []
    ins_list = []
    for section_id in range(N_SECTION):
        outs_list.append(jnp.dot(out_proj[section_id].astype(jnp.float32), finals[section_id].astype(jnp.float32), preferred_element_type=jnp.float32).astype(jnp.bfloat16))
        earlier = finals[(section_id - 1) % N_SECTION]
        ins_list.append(lax.dot_general(earlier.astype(jnp.float32), in_proj[section_id].astype(jnp.float32), (((0,), (0,)), ((), ())), preferred_element_type=jnp.float32).astype(jnp.bfloat16))
    return (jnp.stack(outs_list), jnp.stack(ins_list))
```

```python
import functools

import jax
import jax.numpy as jnp
from jax import lax
from jax.experimental import pallas as pl
from jax.experimental.pallas import tpu as pltpu
from jax.sharding import PartitionSpec as P

B = 128
F32, BF16 = jnp.float32, jnp.bfloat16
HIGH = lax.Precision.HIGHEST
GATHER_LIMIT = 16 << 20


def passed_along(value, axis, steps):
    count = lax.axis_size(axis)
    pairs = [(source, (source + steps) % count) for source in range(count)]
    return lax.ppermute(value, axis, pairs)


def nn(a, b, **kw):
    return lax.dot_general(a, b, (((1,), (0,)), ((), ())), preferred_element_type=F32, **kw)


def nt(a, b, **kw):
    return lax.dot_general(a, b, (((1,), (1,)), ((), ())), preferred_element_type=F32, **kw)


def lane_of(x, j):
    return jnp.take_along_axis(x, jnp.full((8, B), j, jnp.int32), axis=1)


def row_of(x, s):
    return jnp.broadcast_to(x[s : s + 1, :], (8, B))


def factor_core(V):
    n = len(V)
    sub = lax.broadcasted_iota(jnp.int32, (8, B), 0)
    lane = lax.broadcasted_iota(jnp.int32, (8, B), 1)
    out = []
    for p in range(n):
        in_panel = (lane >= 8 * p) & (lane < 8 * p + 8)
        C = [lane_of(V[p], 8 * p + j) for j in range(8)]
        below = {i: [lane_of(V[i], 8 * p + j) for j in range(8)] for i in range(p + 1, n)}
        X = jnp.where(in_panel, (lane - 8 * p == sub).astype(F32), V[p])
        U = X
        pivots = jnp.ones((8, B), F32)
        for j in range(8):
            d = row_of(C[j], j)
            inv = 1.0 / d
            pivots = jnp.where(sub == j, d, pivots)
            own = sub == j
            for k in range(j + 1, 8):
                s = row_of(C[k], j) * inv
                C[k] = jnp.where(own, s, C[k] - C[j] * s)
            x = row_of(X, j) * inv
            X = jnp.where(own, x, X - C[j] * x)
            if j < 7:
                U = U - jnp.where(sub > j, C[j] * inv, 0.0) * row_of(U, j)
        row = sub + 8 * p
        out.append(jnp.where(lane <= row, U * lax.rsqrt(pivots), 0.0))
        for i in range(p + 1, n):
            t = [below[i][j] * row_of(X, j) for j in range(8)]
            V[i] = jnp.where(in_panel, 0.0, V[i]) - (
                ((t[0] + t[1]) + (t[2] + t[3])) + ((t[4] + t[5]) + (t[6] + t[7]))
            )
    return out


def factor(g_ref, w_ref, l_ref):
    n = g_ref.shape[0]
    for k in range(0, n, B):
        rows = factor_core([g_ref[k + 8 * i : k + 8 * i + 8, k : k + B] for i in range(B // 8)])
        for i, row in enumerate(rows):
            w_ref[k + 8 * i : k + 8 * i + 8, k : k + B] = row
        w = w_ref[k : k + B, k : k + B]
        if k + B < n:
            l_ref[k + B :, k : k + B] = nt(g_ref[k + B :, k : k + B], w, precision=HIGH)
            for m in range(k + B, n, B):
                g_ref[m:, m : m + B] -= nt(
                    l_ref[m:, k : k + B], l_ref[m : m + B, k : k + B], precision=HIGH
                )
            w_ref[k : k + B, k + B :] = jnp.zeros((B, n - k - B), F32)
        if k:
            e = nn(l_ref[k : k + B, :k], w_ref[:k, :k], precision=HIGH)
            w_ref[k : k + B, :k] = -nn(w, e, precision=HIGH)


def split(x):
    hi = x.astype(BF16)
    return hi, (x - hi.astype(F32)).astype(BF16)


def loop(count, body):
    lax.fori_loop(0, count, lambda i, c: (body(i), c)[1], 0)


def tile(i, size):
    return pl.ds(pl.multiple_of(i * size, size), size)


def finish(hi, lo, gram, w, low, whi, wlo, basis_ref, in_ref, moved_ref):
    dirs, width = hi.shape
    size = 256
    for c in range(0, dirs, size):
        a, b = hi[c : c + size, :], lo[c : c + size, :]
        gram[c:, c : c + size] = nt(hi[c:, :], a) + nt(hi[c:, :], b) + nt(lo[c:, :], a)
    factor(gram, w, low)
    high, rest = split(w[...])
    whi[...] = high
    wlo[...] = rest

    def rows(i):
        d = tile(i, size)
        for c in range(0, dirs, size):
            k = c + size
            a, b = hi[:k, d], lo[:k, d]
            out = nn(whi[c:k, :k], a) + nn(whi[c:k, :k], b) + nn(wlo[c:k, :k], a)
            basis_ref[c:k, d] = out.astype(BF16)

    loop(width // size, rows)
    moved_ref[...] = nn(basis_ref[...], in_ref[...]).astype(BF16)


def gathered_kernel(count, *refs):
    full = (count - 1) // 2
    n_items = 2 * full + 3
    a_items, s_items = refs[:n_items], refs[n_items : 2 * n_items]
    in_any, basis_ref, moved_ref = refs[2 * n_items : 2 * n_items + 3]
    acts, start, proj, hi, lo, gram, w, low, whi, wlo, in_ref, sems = refs[2 * n_items + 3 :]
    dirs, width = start.shape
    tokens = acts.shape[0]
    rows, cols = tokens // count, width // count
    me = lax.axis_index("group")
    pos = jnp.where(me % 2 == 0, me // 2, count - 1 - me // 2)
    copies = [pltpu.make_async_copy(in_any, in_ref, sems.at[0])]
    for n in range(n_items):
        if n < n_items - 2:
            step = 0 if n == 0 else (-n if n <= full else n - full)
            a_rows, s_rows, slot = (0, rows), (0, dirs), n
        else:
            step, slot = count // 2, count - 1
            half = n - (n_items - 2)
            a_rows = (half * (rows // 2), rows // 2)
            s_rows = (half * (dirs // 2), dirs // 2)
        at = lax.rem(pos + step + count, count)
        owner = jnp.where(at < count // 2, 2 * at, 2 * (count - 1 - at) + 1)
        lanes = pl.ds(pl.multiple_of(owner * cols, cols), cols)
        copies.append(
            pltpu.make_async_copy(
                a_items[n], acts.at[pl.ds(slot * rows + a_rows[0], a_rows[1]), :], sems.at[1 + 2 * n]
            )
        )
        copies.append(
            pltpu.make_async_copy(
                s_items[n], start.at[pl.ds(*s_rows), lanes], sems.at[2 + 2 * n]
            )
        )
    for copy in copies:
        copy.start()
    for copy in copies[1:]:
        copy.wait()
    size = 256

    def project(i):
        proj[:, tile(i, size)] = nt(start[...], acts[tile(i, size), :]).astype(BF16)

    def cover(i):
        high, rest = split(nn(proj[...], acts[:, tile(i, size)]))
        hi[:, tile(i, size)] = high
        lo[:, tile(i, size)] = rest

    loop(tokens // size, project)
    loop(width // size, cover)
    copies[0].wait()
    finish(hi, lo, gram, w, low, whi, wlo, basis_ref, in_ref, moved_ref)


def image_kernel(image_any, in_any, basis_ref, moved_ref, part, hi, lo, gram, w, low, whi, wlo, in_ref, sems):
    copy = pltpu.make_async_copy(in_any, in_ref, sems.at[0])
    copy.start()

    def taken(i):
        c = pltpu.make_async_copy(image_any.at[:, tile(i, part.shape[1])], part, sems.at[1])
        c.start()
        c.wait()
        high, rest = split(part[...])
        hi[:, tile(i, part.shape[1])] = high
        lo[:, tile(i, part.shape[1])] = rest

    loop(hi.shape[1] // part.shape[1], taken)
    copy.wait()
    finish(hi, lo, gram, w, low, whi, wlo, basis_ref, in_ref, moved_ref)


def work_scratch(dirs, width, in_shape):
    return [
        pltpu.VMEM((dirs, width), BF16),
        pltpu.VMEM((dirs, width), BF16),
        pltpu.VMEM((dirs, dirs), F32),
        pltpu.VMEM((dirs, dirs), F32),
        pltpu.VMEM((dirs, dirs), F32),
        pltpu.VMEM((dirs, dirs), BF16),
        pltpu.VMEM((dirs, dirs), BF16),
        pltpu.VMEM(in_shape, BF16),
    ]


def ring_items(own, perms, count, cut):
    forward, backward = perms
    behind, ahead = [own], [own]
    for _ in range((count - 1) // 2):
        behind.append(lax.ppermute(behind[-1], "group", forward))
        ahead.append(lax.ppermute(ahead[-1], "group", backward))
    last = [
        lax.ppermute(behind[-1][:cut], "group", forward),
        lax.ppermute(ahead[-1][cut:], "group", backward),
    ]
    return behind + ahead[1:] + last


def per_device(acts, start_basis, out_proj, in_proj):
    tokens, width = acts[0], acts.shape[2]
    dirs = start_basis.shape[2]
    count = lax.axis_size("group")
    in_next = passed_along(in_proj[0], "section", -1)
    out_shape = (
        jax.ShapeDtypeStruct((dirs, width), BF16),
        jax.ShapeDtypeStruct((dirs, in_next.shape[1]), BF16),
    )
    scratch = work_scratch(dirs, width, in_next.shape)
    n_tokens = count * tokens.shape[0]
    hbm = pl.BlockSpec(memory_space=pl.ANY)
    params = pltpu.CompilerParams(vmem_limit_bytes=56 << 20)
    if count % 2 == 0 and n_tokens * width * 2 <= GATHER_LIMIT and (width // count) % B == 0:
        order = list(range(0, count, 2)) + list(range(count - 1, 0, -2))
        forward = [(order[i], order[(i + 1) % count]) for i in range(count)]
        perms = (forward, [(b, a) for a, b in forward])
        a_items = ring_items(tokens, perms, count, tokens.shape[0] // 2)
        s_items = ring_items(start_basis[0].T.astype(BF16), perms, count, dirs // 2)
        basis, moved = pl.pallas_call(
            functools.partial(gathered_kernel, count),
            out_shape=out_shape,
            in_specs=[hbm] * (2 * len(a_items) + 1),
            scratch_shapes=[
                pltpu.VMEM((n_tokens, width), BF16),
                pltpu.VMEM((dirs, width), BF16),
                pltpu.VMEM((dirs, n_tokens), BF16),
            ]
            + scratch
            + [pltpu.SemaphoreType.DMA((2 * len(a_items) + 1,))],
            compiler_params=params,
        )(*a_items, *s_items, in_next)
    else:
        lowered = lax.all_gather(start_basis[0].astype(BF16), "group", axis=0, tiled=True)
        projected = jnp.dot(tokens, lowered, preferred_element_type=F32).astype(BF16)
        partial = lax.dot_general(
            tokens, projected, (((0,), (0,)), ((), ())), preferred_element_type=F32
        )
        part = lax.psum_scatter(partial, "group", scatter_dimension=0, tiled=True)
        image = lax.all_gather(part, "group", axis=0, tiled=True)
        basis, moved = pl.pallas_call(
            image_kernel,
            out_shape=out_shape,
            in_specs=[hbm, hbm],
            scratch_shapes=[pltpu.VMEM((dirs, 256), F32)]
            + scratch
            + [pltpu.SemaphoreType.DMA((2,))],
            compiler_params=params,
        )(image.T, in_next)
    rotated_in = passed_along(moved, "section", 1)
    rotated_out = nt(out_proj[0], basis).astype(BF16)
    return (rotated_out[None], rotated_in[None])


def solution(mesh):
    in_specs = (
        P("section", "group", None),
        P("section", "group", None),
        P("section", "group", None),
        P("section", None, "group"),
    )
    out_specs = (P("section", "group", None), P("section", None, "group"))
    return jax.shard_map(
        per_device, mesh=mesh, in_specs=in_specs, out_specs=out_specs, check_vma=False
    )
```

```python
import functools

import jax
import jax.numpy as jnp
from jax import lax
from jax.experimental import pallas as pl
from jax.experimental.pallas import tpu as pltpu
from jax.sharding import PartitionSpec as P

B = 128
F32, BF16 = jnp.float32, jnp.bfloat16
HIGH = lax.Precision.HIGHEST
GATHER_LIMIT = 16 << 20


def passed_along(value, axis, steps):
    count = lax.axis_size(axis)
    pairs = [(source, (source + steps) % count) for source in range(count)]
    return lax.ppermute(value, axis, pairs)


def nn(a, b, **kw):
    return lax.dot_general(a, b, (((1,), (0,)), ((), ())), preferred_element_type=F32, **kw)


def nt(a, b, **kw):
    return lax.dot_general(a, b, (((1,), (1,)), ((), ())), preferred_element_type=F32, **kw)


def lane_of(x, j):
    return jnp.take_along_axis(x, jnp.full((8, B), j, jnp.int32), axis=1)


def row_of(x, s):
    return jnp.broadcast_to(x[s : s + 1, :], (8, B))


def factor_core(V):
    n = len(V)
    sub = lax.broadcasted_iota(jnp.int32, (8, B), 0)
    lane = lax.broadcasted_iota(jnp.int32, (8, B), 1)
    out = []
    for p in range(n):
        in_panel = (lane >= 8 * p) & (lane < 8 * p + 8)
        C = [lane_of(V[p], 8 * p + j) for j in range(8)]
        below = {i: [lane_of(V[i], 8 * p + j) for j in range(8)] for i in range(p + 1, n)}
        X = jnp.where(in_panel, (lane - 8 * p == sub).astype(F32), V[p])
        U = X
        pivots = jnp.ones((8, B), F32)
        for j in range(8):
            d = row_of(C[j], j)
            inv = 1.0 / d
            pivots = jnp.where(sub == j, d, pivots)
            own = sub == j
            for k in range(j + 1, 8):
                s = row_of(C[k], j) * inv
                C[k] = jnp.where(own, s, C[k] - C[j] * s)
            x = row_of(X, j) * inv
            X = jnp.where(own, x, X - C[j] * x)
            if j < 7:
                U = U - jnp.where(sub > j, C[j] * inv, 0.0) * row_of(U, j)
        row = sub + 8 * p
        out.append(jnp.where(lane <= row, U * lax.rsqrt(pivots), 0.0))
        for i in range(p + 1, n):
            t = [below[i][j] * row_of(X, j) for j in range(8)]
            V[i] = jnp.where(in_panel, 0.0, V[i]) - (
                ((t[0] + t[1]) + (t[2] + t[3])) + ((t[4] + t[5]) + (t[6] + t[7]))
            )
    return out


def split(x):
    hi = x.astype(BF16)
    return hi, (x - hi.astype(F32)).astype(BF16)


def loop(count, body):
    lax.fori_loop(0, count, lambda i, c: (body(i), c)[1], 0)


def tile(i, size):
    return pl.ds(pl.multiple_of(i * size, size), size)


def three(dot, a, b):
    return dot(a[0], b[0]) + dot(a[0], b[1]) + dot(a[1], b[0])


def invert(diag, w):
    for i, row in enumerate(factor_core([diag[8 * i : 8 * i + 8, :] for i in range(B // 8)])):
        w[8 * i : 8 * i + 8, :] = row


def finish(hi, lo, gram, lhi, llo, qhi, qlo, cols, base, diag, w, in_ref, op_ref, moved_ref, out_ref):
    dirs, width = hi.shape
    n, size = dirs // B, 256
    for c in range(0, dirs, size):
        a, b = hi[c : c + size, :], lo[c : c + size, :]
        gram[c:, c : c + size] = nt(hi[c:, :], a) + nt(hi[c:, :], b) + nt(lo[c:, :], a)
    for ref in (lhi, llo, qhi, qlo):
        ref[...] = jnp.zeros(ref.shape, ref.dtype)

    def results(k, winv):
        mine = tile(k, B)
        la = lhi[mine, :], llo[mine, :]
        wa = split(winv)
        for d in range(0, width, size):
            t = hi[mine, d : d + size].astype(F32) + lo[mine, d : d + size].astype(F32)
            t = t - three(nn, la, (qhi[:, d : d + size], qlo[:, d : d + size]))
            high, rest = split(three(nn, wa, split(t)))
            qhi[mine, d : d + size] = high
            qlo[mine, d : d + size] = rest
        low = qhi[mine, :]
        for r in range(0, op_ref.shape[0], size):
            if r + size <= op_ref.shape[0]:
                rows = slice(r, r + size)
            else:
                rows = slice(r, op_ref.shape[0])
            out_ref[rows, mine] = nt(op_ref[rows, :], low).astype(BF16)
        moved_ref[mine, :] = nn(low, in_ref[...]).astype(BF16)

    def chain(k, column, ahead):
        invert(diag, w.at[lax.rem(k, 2)])
        part = nt(column[tile(ahead, B), :], w[lax.rem(k, 2)], precision=HIGH)
        diag[...] = base[tile(ahead, B), :] - nt(part, part, precision=HIGH)

    diag[...] = gram[:B, :B]
    cols[0] = gram[:, :B]
    base[...] = gram[:, B : 2 * B]
    chain(jnp.int32(0), cols.at[0], jnp.int32(1))
    row = lax.broadcasted_iota(jnp.int32, (dirs, B), 0)

    def step(i):
        k = i + 1
        now, then = lax.rem(k, 2), lax.rem(k + 1, 2)
        ahead = jnp.minimum(k + 1, n - 1)
        winv = w[then]
        left = jnp.where(row >= k * B, nt(cols[then], winv, precision=HIGH), 0.0)
        high, rest = split(left)
        lhi[:, tile(k - 1, B)] = high
        llo[:, tile(k - 1, B)] = rest
        mine = tile(k, B)
        cols[now] = base[...] - three(
            nt, (high, rest), (lhi[mine, tile(k - 1, B)], llo[mine, tile(k - 1, B)])
        )
        nxt = tile(ahead, B)
        base[...] = gram[:, nxt] - three(
            nt, (lhi[...], llo[...]), (lhi[nxt, :], llo[nxt, :])
        )
        results(k - 1, winv)
        chain(k, cols.at[now], ahead)

    loop(n - 1, step)
    results(jnp.int32(n - 1), w[(n - 1) % 2])


def gathered_kernel(count, *refs):
    full = (count - 1) // 2
    n_items = 2 * full + 3
    a_items, s_items = refs[:n_items], refs[n_items : 2 * n_items]
    in_any, op_any, moved_ref, out_ref = refs[2 * n_items : 2 * n_items + 4]
    acts, start, proj, hi, lo, *work, in_ref, op_ref, sems = refs[2 * n_items + 4 :]
    dirs, width = start.shape
    tokens = acts.shape[0]
    rows, cols = tokens // count, width // count
    me = lax.axis_index("group")
    pos = jnp.where(me % 2 == 0, me // 2, count - 1 - me // 2)
    copies = [
        pltpu.make_async_copy(in_any, in_ref, sems.at[0]),
        pltpu.make_async_copy(op_any, op_ref, sems.at[1]),
    ]
    for n in range(n_items):
        if n < n_items - 2:
            step = 0 if n == 0 else (-n if n <= full else n - full)
            a_rows, s_rows, slot = (0, rows), (0, dirs), n
        else:
            step, slot = count // 2, count - 1
            half = n - (n_items - 2)
            a_rows = (half * (rows // 2), rows // 2)
            s_rows = (half * (dirs // 2), dirs // 2)
        at = lax.rem(pos + step + count, count)
        owner = jnp.where(at < count // 2, 2 * at, 2 * (count - 1 - at) + 1)
        lanes = pl.ds(pl.multiple_of(owner * cols, cols), cols)
        copies.append(
            pltpu.make_async_copy(
                a_items[n], acts.at[pl.ds(slot * rows + a_rows[0], a_rows[1]), :], sems.at[2 + 2 * n]
            )
        )
        copies.append(
            pltpu.make_async_copy(
                s_items[n], start.at[pl.ds(*s_rows), lanes], sems.at[3 + 2 * n]
            )
        )
    for copy in copies[2:] + copies[:2]:
        copy.start()
    for copy in copies[2:]:
        copy.wait()
    size = 256

    def project(i):
        proj[:, tile(i, size)] = nt(start[...], acts[tile(i, size), :]).astype(BF16)

    def cover(i):
        high, rest = split(nn(proj[...], acts[:, tile(i, size)]))
        hi[:, tile(i, size)] = high
        lo[:, tile(i, size)] = rest

    loop(tokens // size, project)
    loop(width // size, cover)
    for copy in copies[:2]:
        copy.wait()
    finish(hi, lo, *work, in_ref, op_ref, moved_ref, out_ref)


def image_kernel(image_any, in_any, op_any, moved_ref, out_ref, part, hi, lo, *rest):
    *work, in_ref, op_ref, sems = rest
    copies = [
        pltpu.make_async_copy(in_any, in_ref, sems.at[0]),
        pltpu.make_async_copy(op_any, op_ref, sems.at[1]),
    ]
    for copy in copies:
        copy.start()

    def taken(i):
        c = pltpu.make_async_copy(image_any.at[:, tile(i, part.shape[1])], part, sems.at[2])
        c.start()
        c.wait()
        high, low = split(part[...])
        hi[:, tile(i, part.shape[1])] = high
        lo[:, tile(i, part.shape[1])] = low

    loop(hi.shape[1] // part.shape[1], taken)
    for copy in copies:
        copy.wait()
    finish(hi, lo, *work, in_ref, op_ref, moved_ref, out_ref)


def work_scratch(dirs, width, in_shape, op_shape):
    return [
        pltpu.VMEM((dirs, width), BF16),
        pltpu.VMEM((dirs, width), BF16),
        pltpu.VMEM((dirs, dirs), F32),
        pltpu.VMEM((dirs, dirs), BF16),
        pltpu.VMEM((dirs, dirs), BF16),
        pltpu.VMEM((dirs, width), BF16),
        pltpu.VMEM((dirs, width), BF16),
        pltpu.VMEM((2, dirs, B), F32),
        pltpu.VMEM((dirs, B), F32),
        pltpu.VMEM((B, B), F32),
        pltpu.VMEM((2, B, B), F32),
        pltpu.VMEM(in_shape, BF16),
        pltpu.VMEM(op_shape, BF16),
    ]


def ring_items(own, perms, count, cut):
    forward, backward = perms
    behind, ahead = [own], [own]
    for _ in range((count - 1) // 2):
        behind.append(lax.ppermute(behind[-1], "group", forward))
        ahead.append(lax.ppermute(ahead[-1], "group", backward))
    last = [
        lax.ppermute(behind[-1][:cut], "group", forward),
        lax.ppermute(ahead[-1][cut:], "group", backward),
    ]
    return behind + ahead[1:] + last


def per_device(acts, start_basis, out_proj, in_proj):
    tokens, width = acts[0], acts.shape[2]
    dirs = start_basis.shape[2]
    count = lax.axis_size("group")
    in_next = passed_along(in_proj[0], "section", -1)
    out_shape = (
        jax.ShapeDtypeStruct((dirs, in_next.shape[1]), BF16),
        jax.ShapeDtypeStruct((out_proj.shape[1], dirs), BF16),
    )
    scratch = work_scratch(dirs, width, in_next.shape, out_proj[0].shape)
    n_tokens = count * tokens.shape[0]
    hbm = pl.BlockSpec(memory_space=pl.ANY)
    params = pltpu.CompilerParams(vmem_limit_bytes=56 << 20)
    if count % 2 == 0 and n_tokens * width * 2 <= GATHER_LIMIT and (width // count) % B == 0:
        order = list(range(0, count, 2)) + list(range(count - 1, 0, -2))
        forward = [(order[i], order[(i + 1) % count]) for i in range(count)]
        perms = (forward, [(b, a) for a, b in forward])
        a_items = ring_items(tokens, perms, count, tokens.shape[0] // 2)
        s_items = ring_items(start_basis[0].T.astype(BF16), perms, count, dirs // 2)
        moved, rotated_out = pl.pallas_call(
            functools.partial(gathered_kernel, count),
            out_shape=out_shape,
            in_specs=[hbm] * (2 * len(a_items) + 2),
            scratch_shapes=[
                pltpu.VMEM((n_tokens, width), BF16),
                pltpu.VMEM((dirs, width), BF16),
                pltpu.VMEM((dirs, n_tokens), BF16),
            ]
            + scratch
            + [pltpu.SemaphoreType.DMA((2 * len(a_items) + 2,))],
            compiler_params=params,
        )(*a_items, *s_items, in_next, out_proj[0])
    else:
        lowered = lax.all_gather(start_basis[0].astype(BF16), "group", axis=0, tiled=True)
        projected = jnp.dot(tokens, lowered, preferred_element_type=F32).astype(BF16)
        partial = lax.dot_general(
            tokens, projected, (((0,), (0,)), ((), ())), preferred_element_type=F32
        )
        part = lax.psum_scatter(partial, "group", scatter_dimension=0, tiled=True)
        image = lax.all_gather(part, "group", axis=0, tiled=True)
        moved, rotated_out = pl.pallas_call(
            image_kernel,
            out_shape=out_shape,
            in_specs=[hbm] * 3,
            scratch_shapes=[pltpu.VMEM((dirs, 256), F32)]
            + scratch
            + [pltpu.SemaphoreType.DMA((3,))],
            compiler_params=params,
        )(image.T, in_next, out_proj[0])
    rotated_in = passed_along(moved, "section", 1)
    return (rotated_out[None], rotated_in[None])


def solution(mesh):
    in_specs = (
        P("section", "group", None),
        P("section", "group", None),
        P("section", "group", None),
        P("section", None, "group"),
    )
    out_specs = (P("section", "group", None), P("section", None, "group"))
    return jax.shard_map(
        per_device, mesh=mesh, in_specs=in_specs, out_specs=out_specs, check_vma=False
    )
```

```python
import functools

import jax
import jax.numpy as jnp
from jax import lax
from jax.experimental import pallas as pl
from jax.experimental.pallas import tpu as pltpu
from jax.sharding import PartitionSpec as P

B = 128
F32, BF16 = jnp.float32, jnp.bfloat16
HIGH = lax.Precision.HIGHEST
GATHER_LIMIT = 16 << 20


def passed_along(value, axis, steps):
    count = lax.axis_size(axis)
    pairs = [(source, (source + steps) % count) for source in range(count)]
    return lax.ppermute(value, axis, pairs)


def nn(a, b, **kw):
    return lax.dot_general(a, b, (((1,), (0,)), ((), ())), preferred_element_type=F32, **kw)


def nt(a, b, **kw):
    return lax.dot_general(a, b, (((1,), (1,)), ((), ())), preferred_element_type=F32, **kw)


def lane_of(x, j):
    return jnp.take_along_axis(x, jnp.full((8, B), j, jnp.int32), axis=1)


def row_of(x, s):
    return jnp.broadcast_to(x[s : s + 1, :], (8, B))


def factor_core(V):
    n = len(V)
    sub = lax.broadcasted_iota(jnp.int32, (8, B), 0)
    lane = lax.broadcasted_iota(jnp.int32, (8, B), 1)
    out = []
    for p in range(n):
        in_panel = (lane >= 8 * p) & (lane < 8 * p + 8)
        C = [lane_of(V[p], 8 * p + j) for j in range(8)]
        below = {i: [lane_of(V[i], 8 * p + j) for j in range(8)] for i in range(p + 1, n)}
        X = jnp.where(in_panel, (lane - 8 * p == sub).astype(F32), V[p])
        U = X
        pivots = jnp.ones((8, B), F32)
        for j in range(8):
            d = row_of(C[j], j)
            inv = 1.0 / d
            pivots = jnp.where(sub == j, d, pivots)
            own = sub == j
            for k in range(j + 1, 8):
                s = row_of(C[k], j) * inv
                C[k] = jnp.where(own, s, C[k] - C[j] * s)
            x = row_of(X, j) * inv
            X = jnp.where(own, x, X - C[j] * x)
            if j < 7:
                U = U - jnp.where(sub > j, C[j] * inv, 0.0) * row_of(U, j)
        row = sub + 8 * p
        out.append(jnp.where(lane <= row, U * lax.rsqrt(pivots), 0.0))
        for i in range(p + 1, n):
            t = [below[i][j] * row_of(X, j) for j in range(8)]
            V[i] = jnp.where(in_panel, 0.0, V[i]) - (
                ((t[0] + t[1]) + (t[2] + t[3])) + ((t[4] + t[5]) + (t[6] + t[7]))
            )
    return out


def split(x):
    hi = x.astype(BF16)
    return hi, (x - hi.astype(F32)).astype(BF16)


def loop(count, body):
    lax.fori_loop(0, count, lambda i, c: (body(i), c)[1], 0)


def tile(i, size):
    return pl.ds(pl.multiple_of(i * size, size), size)


def three(dot, a, b):
    return dot(a[0], b[0]) + dot(a[0], b[1]) + dot(a[1], b[0])


def factor_block(diag, w):
    for i, row in enumerate(factor_core([diag[8 * i : 8 * i + 8, :] for i in range(B // 8)])):
        w[8 * i : 8 * i + 8, :] = row


def finish(hi, lo, gram, lhi, llo, wcat, whi, wlo, fb, cols, base, diag, wd, in_ref, op_ref, moved_ref, out_ref):
    dirs, width = hi.shape
    n, size = dirs // B, 2 * B
    for c in range(0, dirs, size):
        a, b = hi[c : c + size, :], lo[c : c + size, :]
        gram[c:, c : c + size] = nt(hi[c:, :], a) + nt(hi[c:, :], b) + nt(lo[c:, :], a)
    for ref in (lhi, llo, whi, wlo, wd):
        ref[...] = jnp.zeros(ref.shape, ref.dtype)
    cols[1] = jnp.zeros((dirs, B), F32)
    base[...] = gram[:, :B]
    diag[...] = gram[:B, :B]
    row = lax.broadcasted_iota(jnp.int32, (dirs, B), 0)

    def inverse_rows(c):
        mine = tile(c, size)
        first, second = tile(2 * c, B), tile(2 * c + 1, B)
        wa, wb = split(wd[2 * c]), split(wd[2 * c + 1])
        between = three(nn, (lhi[second, first], llo[second, first]), wa)
        wab = -three(nn, wb, split(between))
        zero = jnp.zeros((B, B), F32)
        inv = split(
            jnp.concatenate(
                [
                    jnp.concatenate([wd[2 * c], zero], axis=1),
                    jnp.concatenate([wab, wd[2 * c + 1]], axis=1),
                ],
                axis=0,
            )
        )
        e = three(nn, (lhi[mine, :], llo[mine, :]), (whi[...], wlo[...]))
        high, rest = split(-three(nn, inv, split(e)))
        for ref, value, own in ((whi, high, inv[0]), (wlo, rest, inv[1])):
            ref[mine, :] = value
            ref[mine, mine] = own
        wcat[:size, :] = whi[mine, :]
        wcat[size:, :] = wlo[mine, :]

    def basis_rows(lanes):
        for d in lanes:
            both = nn(wcat[...], hi[:, d : d + size])
            one = nn(wcat[:size, :], lo[:, d : d + size])
            fb[:, d : d + size] = (both[:size] + both[size:] + one).astype(BF16)

    def products(c):
        mine = tile(c, size)
        half = op_ref.shape[0] // 2
        for r in (0, half):
            out_ref[r : r + half, mine] = nt(op_ref[r : r + half, :], fb[...]).astype(BF16)
        moved_ref[mine, :] = nn(fb[...], in_ref[...]).astype(BF16)

    def block(k, now, beside):
        then = 1 - now
        before, ahead = jnp.maximum(k - 1, 0), jnp.minimum(k + 1, n - 1)
        last, mine, nxt = tile(before, B), tile(k, B), tile(ahead, B)
        left = three(nt, split(cols[then]), split(wd[before]))
        high, rest = split(jnp.where(row >= k * B, left, 0.0))
        lhi[:, last] = high
        llo[:, last] = rest
        cols[now] = base[...] - three(nt, (high, rest), (lhi[mine, last], llo[mine, last]))
        base[...] = gram[:, nxt] - three(nt, (lhi[...], llo[...]), (lhi[nxt, :], llo[nxt, :]))
        beside()
        factor_block(diag, wd.at[k])
        part = split(three(nt, split(cols[now, nxt, :]), split(wd[k])))
        diag[...] = base[nxt, :] - three(nt, part, part)

    middle = width // (2 * size) * size
    front, back = range(0, middle, size), range(middle, width, size)

    def step(b):
        c = jnp.maximum(b - 1, 0)

        def one():
            inverse_rows(c)
            basis_rows(front)

        def two():
            basis_rows(back)
            products(c)

        block(2 * b, 0, one)
        block(2 * b + 1, 1, two)

    loop(n // 2, step)
    last = jnp.int32(n // 2 - 1)
    inverse_rows(last)
    basis_rows(front)
    basis_rows(back)
    products(last)


def gathered_kernel(count, *refs):
    full = (count - 1) // 2
    n_items = 2 * full + 3
    a_items, s_items = refs[:n_items], refs[n_items : 2 * n_items]
    in_any, op_any, moved_ref, out_ref = refs[2 * n_items : 2 * n_items + 4]
    acts, start, proj, hi, lo, *work, in_ref, op_ref, sems = refs[2 * n_items + 4 :]
    dirs, width = start.shape
    tokens = acts.shape[0]
    rows, cols = tokens // count, width // count
    me = lax.axis_index("group")
    pos = jnp.where(me % 2 == 0, me // 2, count - 1 - me // 2)
    copies = [
        pltpu.make_async_copy(in_any, in_ref, sems.at[0]),
        pltpu.make_async_copy(op_any, op_ref, sems.at[1]),
    ]
    for n in range(n_items):
        if n < n_items - 2:
            step = 0 if n == 0 else (-n if n <= full else n - full)
            a_rows, s_rows, slot = (0, rows), (0, dirs), n
        else:
            step, slot = count // 2, count - 1
            half = n - (n_items - 2)
            a_rows = (half * (rows // 2), rows // 2)
            s_rows = (half * (dirs // 2), dirs // 2)
        at = lax.rem(pos + step + count, count)
        owner = jnp.where(at < count // 2, 2 * at, 2 * (count - 1 - at) + 1)
        lanes = pl.ds(pl.multiple_of(owner * cols, cols), cols)
        copies.append(
            pltpu.make_async_copy(
                a_items[n], acts.at[pl.ds(slot * rows + a_rows[0], a_rows[1]), :], sems.at[2 + 2 * n]
            )
        )
        copies.append(
            pltpu.make_async_copy(
                s_items[n], start.at[pl.ds(*s_rows), lanes], sems.at[3 + 2 * n]
            )
        )
    for copy in copies[2:] + copies[:2]:
        copy.start()
    for copy in copies[2:]:
        copy.wait()
    size = 256

    def project(i):
        proj[:, tile(i, size)] = nt(start[...], acts[tile(i, size), :]).astype(BF16)

    def cover(i):
        high, rest = split(nn(proj[...], acts[:, tile(i, size)]))
        hi[:, tile(i, size)] = high
        lo[:, tile(i, size)] = rest

    loop(tokens // size, project)
    loop(width // size, cover)
    for copy in copies[:2]:
        copy.wait()
    finish(hi, lo, *work, in_ref, op_ref, moved_ref, out_ref)


def image_kernel(image_any, in_any, op_any, moved_ref, out_ref, part, hi, lo, *rest):
    *work, in_ref, op_ref, sems = rest
    copies = [
        pltpu.make_async_copy(in_any, in_ref, sems.at[0]),
        pltpu.make_async_copy(op_any, op_ref, sems.at[1]),
    ]
    for copy in copies:
        copy.start()

    def taken(i):
        c = pltpu.make_async_copy(image_any.at[:, tile(i, part.shape[1])], part, sems.at[2])
        c.start()
        c.wait()
        high, low = split(part[...])
        hi[:, tile(i, part.shape[1])] = high
        lo[:, tile(i, part.shape[1])] = low

    loop(hi.shape[1] // part.shape[1], taken)
    for copy in copies:
        copy.wait()
    finish(hi, lo, *work, in_ref, op_ref, moved_ref, out_ref)


def work_scratch(dirs, width, in_shape, op_shape):
    square = pltpu.VMEM((dirs, dirs), BF16)
    return [
        pltpu.VMEM((dirs, width), BF16),
        pltpu.VMEM((dirs, width), BF16),
        pltpu.VMEM((dirs, dirs), F32),
        square,
        square,
        pltpu.VMEM((4 * B, dirs), BF16),
        square,
        square,
        pltpu.VMEM((2 * B, width), BF16),
        pltpu.VMEM((2, dirs, B), F32),
        pltpu.VMEM((dirs, B), F32),
        pltpu.VMEM((B, B), F32),
        pltpu.VMEM((dirs // B, B, B), F32),
        pltpu.VMEM(in_shape, BF16),
        pltpu.VMEM(op_shape, BF16),
    ]


def ring_items(own, perms, count, cut):
    forward, backward = perms
    behind, ahead = [own], [own]
    for _ in range((count - 1) // 2):
        behind.append(lax.ppermute(behind[-1], "group", forward))
        ahead.append(lax.ppermute(ahead[-1], "group", backward))
    last = [
        lax.ppermute(behind[-1][:cut], "group", forward),
        lax.ppermute(ahead[-1][cut:], "group", backward),
    ]
    return behind + ahead[1:] + last


def per_device(acts, start_basis, out_proj, in_proj):
    tokens, width = acts[0], acts.shape[2]
    dirs = start_basis.shape[2]
    count = lax.axis_size("group")
    in_next = passed_along(in_proj[0], "section", -1)
    out_shape = (
        jax.ShapeDtypeStruct((dirs, in_next.shape[1]), BF16),
        jax.ShapeDtypeStruct((out_proj.shape[1], dirs), BF16),
    )
    scratch = work_scratch(dirs, width, in_next.shape, out_proj[0].shape)
    n_tokens = count * tokens.shape[0]
    hbm = pl.BlockSpec(memory_space=pl.ANY)
    params = pltpu.CompilerParams(vmem_limit_bytes=56 << 20)
    if count % 2 == 0 and n_tokens * width * 2 <= GATHER_LIMIT and (width // count) % B == 0:
        order = list(range(0, count, 2)) + list(range(count - 1, 0, -2))
        forward = [(order[i], order[(i + 1) % count]) for i in range(count)]
        perms = (forward, [(b, a) for a, b in forward])
        a_items = ring_items(tokens, perms, count, tokens.shape[0] // 2)
        s_items = ring_items(start_basis[0].T.astype(BF16), perms, count, dirs // 2)
        moved, rotated_out = pl.pallas_call(
            functools.partial(gathered_kernel, count),
            out_shape=out_shape,
            in_specs=[hbm] * (2 * len(a_items) + 2),
            scratch_shapes=[
                pltpu.VMEM((n_tokens, width), BF16),
                pltpu.VMEM((dirs, width), BF16),
                pltpu.VMEM((dirs, n_tokens), BF16),
            ]
            + scratch
            + [pltpu.SemaphoreType.DMA((2 * len(a_items) + 2,))],
            compiler_params=params,
        )(*a_items, *s_items, in_next, out_proj[0])
    else:
        lowered = lax.all_gather(start_basis[0].astype(BF16), "group", axis=0, tiled=True)
        projected = jnp.dot(tokens, lowered, preferred_element_type=F32).astype(BF16)
        partial = lax.dot_general(
            tokens, projected, (((0,), (0,)), ((), ())), preferred_element_type=F32
        )
        part = lax.psum_scatter(partial, "group", scatter_dimension=0, tiled=True)
        image = lax.all_gather(part, "group", axis=0, tiled=True)
        moved, rotated_out = pl.pallas_call(
            image_kernel,
            out_shape=out_shape,
            in_specs=[hbm] * 3,
            scratch_shapes=[pltpu.VMEM((dirs, 256), F32)]
            + scratch
            + [pltpu.SemaphoreType.DMA((3,))],
            compiler_params=params,
        )(image.T, in_next, out_proj[0])
    rotated_in = passed_along(moved, "section", 1)
    return (rotated_out[None], rotated_in[None])


def solution(mesh):
    in_specs = (
        P("section", "group", None),
        P("section", "group", None),
        P("section", "group", None),
        P("section", None, "group"),
    )
    out_specs = (P("section", "group", None), P("section", None, "group"))
    return jax.shard_map(
        per_device, mesh=mesh, in_specs=in_specs, out_specs=out_specs, check_vma=False
    )
```

```python
import functools

import jax
import jax.numpy as jnp
from jax import lax
from jax.experimental import pallas as pl
from jax.experimental.pallas import tpu as pltpu
from jax.sharding import PartitionSpec as P

B = 128
F32, BF16 = jnp.float32, jnp.bfloat16
HIGH = lax.Precision.HIGHEST
GATHER_LIMIT = 16 << 20


def passed_along(value, axis, steps):
    count = lax.axis_size(axis)
    pairs = [(source, (source + steps) % count) for source in range(count)]
    return lax.ppermute(value, axis, pairs)


def nn(a, b, **kw):
    return lax.dot_general(a, b, (((1,), (0,)), ((), ())), preferred_element_type=F32, **kw)


def nt(a, b, **kw):
    return lax.dot_general(a, b, (((1,), (1,)), ((), ())), preferred_element_type=F32, **kw)


def lane_of(x, j):
    return jnp.take_along_axis(x, jnp.full((8, B), j, jnp.int32), axis=1)


def row_of(x, s):
    return jnp.broadcast_to(x[s : s + 1, :], (8, B))


def factor_core(V):
    n = len(V)
    sub = lax.broadcasted_iota(jnp.int32, (8, B), 0)
    lane = lax.broadcasted_iota(jnp.int32, (8, B), 1)
    out = []
    for p in range(n):
        in_panel = (lane >= 8 * p) & (lane < 8 * p + 8)
        C = [lane_of(V[p], 8 * p + j) for j in range(8)]
        below = {i: [lane_of(V[i], 8 * p + j) for j in range(8)] for i in range(p + 1, n)}
        X = jnp.where(in_panel, (lane - 8 * p == sub).astype(F32), V[p])
        U = X
        pivots = jnp.ones((8, B), F32)
        d = row_of(C[0], 0)
        for j in range(8):
            inv = 1.0 / d
            pivots = jnp.where(sub == j, d, pivots)
            own, pivot_column = sub == j, C[j]
            if j < 7:
                d = row_of(C[j + 1], j + 1) - (row_of(C[j], j + 1) * row_of(C[j + 1], j)) * inv
            for k in range(j + 1, 8):
                s = row_of(C[k], j) * inv
                C[k] = jnp.where(own, s, C[k] - pivot_column * s)
            x = row_of(X, j) * inv
            X = jnp.where(own, x, X - pivot_column * x)
            if j < 7:
                U = U - jnp.where(sub > j, pivot_column * inv, 0.0) * row_of(U, j)
        row = sub + 8 * p
        out.append(jnp.where(lane <= row, U * lax.rsqrt(pivots), 0.0))
        for i in range(p + 1, n):
            t = [below[i][j] * row_of(X, j) for j in range(8)]
            V[i] = jnp.where(in_panel, 0.0, V[i]) - (
                ((t[0] + t[1]) + (t[2] + t[3])) + ((t[4] + t[5]) + (t[6] + t[7]))
            )
    return out


def split(x):
    hi = x.astype(BF16)
    return hi, (x - hi.astype(F32)).astype(BF16)


def loop(count, body):
    lax.fori_loop(0, count, lambda i, c: (body(i), c)[1], 0)


def tile(i, size):
    start = i * size
    return pl.ds(start if isinstance(start, int) else pl.multiple_of(start, size), size)


def three(dot, a, b):
    return dot(a[0], b[0]) + dot(a[0], b[1]) + dot(a[1], b[0])


def factor_block(diag, w):
    for i, row in enumerate(factor_core([diag[8 * i : 8 * i + 8, :] for i in range(B // 8)])):
        w[8 * i : 8 * i + 8, :] = row


def stacked(pair, high, low):
    size = pair.shape[0] // 2
    both = nn(pair, high)
    return both[:size] + both[size:] + nn(pair[:size], low)


def finish(hi, lo, gram, lhi, llo, ecat, whi, wlo, yhi, ylo, fb, cols, base, diag, wd, in_ref, op_ref, moved_ref, out_ref):
    dirs, width = hi.shape
    n, size = dirs // B, 2 * B
    lanes = range(0, width, size)

    def gram_tile(c):
        a, b = hi[c : c + size, :], lo[c : c + size, :]
        gram[c:, c : c + size] = nt(hi[c:, :], a) + nt(hi[c:, :], b) + nt(lo[c:, :], a)

    gram_tile(0)
    for ref in (lhi, llo, whi, wlo):
        ref[...] = jnp.zeros(ref.shape, ref.dtype)
    cols[0] = gram[:, :B]
    base[...] = gram[:, B:size]
    diag[...] = gram[:B, :B]
    row = lax.broadcasted_iota(jnp.int32, (dirs, B), 0)

    def prepare(c):
        mine = tile(c, size)
        high, rest = split(three(nn, (lhi[mine, :], llo[mine, :]), (whi[...], wlo[...])))
        ecat[:size, :] = high
        ecat[size:, :] = rest
        for d in lanes:
            at = slice(d, d + size)
            y = hi[mine, at].astype(F32) + lo[mine, at].astype(F32)
            yhi[:, at], ylo[:, at] = split(y - stacked(ecat[...], hi[:, at], lo[:, at]))

    def results(c, more):
        mine = tile(c, size)
        first, second = tile(2 * c, B), tile(2 * c + 1, B)
        wa, wb = split(wd[2 * c]), split(wd[2 * c + 1])
        between = three(nn, (lhi[second, first], llo[second, first]), wa)
        wab = -three(nn, wb, split(between))
        top = jnp.concatenate([wd[2 * c], jnp.zeros((B, B), F32)], axis=1)
        inv = split(jnp.concatenate([top, jnp.concatenate([wab, wd[2 * c + 1]], axis=1)], axis=0))
        pair = jnp.concatenate(inv, axis=0)
        if more:
            rows = split(-three(nn, inv, (ecat[:size, :], ecat[size:, :])))
            for ref, value, own in zip((whi, wlo), rows, inv):
                ref[mine, :] = value
                ref[mine, mine] = own
        for d in lanes:
            at = slice(d, d + size)
            fb[:, at] = stacked(pair, yhi[:, at], ylo[:, at]).astype(BF16)
        moved_ref[mine, :] = nn(fb[...], in_ref[...]).astype(BF16)
        half = op_ref.shape[0] // 2
        for r in (0, half):
            out_ref[r : r + half, mine] = nt(op_ref[r : r + half, :], fb[...]).astype(BF16)

    def block(k, now, beside):
        then = 1 - now
        ahead = jnp.minimum(k + 1, n - 1)
        mine, nxt = tile(k, B), tile(ahead, B)
        if not (isinstance(k, int) and k == 0):
            last = tile(k - 1, B)
            left = three(nt, split(cols[then]), split(wd[k - 1]))
            high, rest = split(jnp.where(row >= k * B, left, 0.0))
            lhi[:, last] = high
            llo[:, last] = rest
            cols[now] = base[...] - three(nt, (high, rest), (lhi[mine, last], llo[mine, last]))
            base[...] = gram[:, nxt] - three(nt, (lhi[...], llo[...]), (lhi[nxt, :], llo[nxt, :]))
        beside()
        factor_block(diag, wd.at[k])
        part = split(three(nt, split(cols[now, nxt, :]), split(wd[k])))
        diag[...] = base[nxt, :] - three(nt, part, part)

    def other_tiles():
        for c in range(2 * size, dirs, size):
            gram_tile(c)
        ecat[...] = jnp.zeros(ecat.shape, BF16)
        yhi[...] = hi[:size, :]
        ylo[...] = lo[:size, :]

    def step(i):
        b = i + 1
        block(2 * b, 0, lambda: results(b - 1, True))
        block(2 * b + 1, 1, lambda: prepare(b))

    block(0, 0, lambda: gram_tile(size))
    block(1, 1, other_tiles)
    loop(n // 2 - 1, step)
    results(jnp.int32(n // 2 - 1), False)


def gathered_kernel(count, *refs):
    full = (count - 1) // 2
    n_items = 2 * full + 3
    a_items, s_items = refs[:n_items], refs[n_items : 2 * n_items]
    in_any, op_any, moved_ref, out_ref = refs[2 * n_items : 2 * n_items + 4]
    acts, start, proj, hi, lo, *work, in_ref, op_ref, sems = refs[2 * n_items + 4 :]
    dirs, width = start.shape
    tokens = acts.shape[0]
    rows, cols = tokens // count, width // count
    me = lax.axis_index("group")
    pos = jnp.where(me % 2 == 0, me // 2, count - 1 - me // 2)
    copies = [
        pltpu.make_async_copy(in_any, in_ref, sems.at[0]),
        pltpu.make_async_copy(op_any, op_ref, sems.at[1]),
    ]
    for n in range(n_items):
        if n < n_items - 2:
            step = 0 if n == 0 else (-n if n <= full else n - full)
            a_rows, s_rows, slot = (0, rows), (0, dirs), n
        else:
            step, slot = count // 2, count - 1
            half = n - (n_items - 2)
            a_rows = (half * (rows // 2), rows // 2)
            s_rows = (half * (dirs // 2), dirs // 2)
        at = lax.rem(pos + step + count, count)
        owner = jnp.where(at < count // 2, 2 * at, 2 * (count - 1 - at) + 1)
        lanes = pl.ds(pl.multiple_of(owner * cols, cols), cols)
        copies.append(
            pltpu.make_async_copy(
                a_items[n], acts.at[pl.ds(slot * rows + a_rows[0], a_rows[1]), :], sems.at[2 + 2 * n]
            )
        )
        copies.append(
            pltpu.make_async_copy(
                s_items[n], start.at[pl.ds(*s_rows), lanes], sems.at[3 + 2 * n]
            )
        )
    for copy in copies[2:] + copies[:2]:
        copy.start()
    for copy in copies[2:]:
        copy.wait()
    size = 256

    def project(i):
        proj[:, tile(i, size)] = nt(start[...], acts[tile(i, size), :]).astype(BF16)

    def cover(i):
        high, rest = split(nn(proj[...], acts[:, tile(i, size)]))
        hi[:, tile(i, size)] = high
        lo[:, tile(i, size)] = rest

    for i in range(tokens // size):
        project(i)
    for i in range(width // size):
        cover(i)
    for copy in copies[:2]:
        copy.wait()
    finish(hi, lo, *work, in_ref, op_ref, moved_ref, out_ref)


def image_kernel(image_any, in_any, op_any, moved_ref, out_ref, part, hi, lo, *rest):
    *work, in_ref, op_ref, sems = rest
    copies = [
        pltpu.make_async_copy(in_any, in_ref, sems.at[0]),
        pltpu.make_async_copy(op_any, op_ref, sems.at[1]),
    ]
    for copy in copies:
        copy.start()

    def taken(i):
        c = pltpu.make_async_copy(image_any.at[:, tile(i, part.shape[1])], part, sems.at[2])
        c.start()
        c.wait()
        high, low = split(part[...])
        hi[:, tile(i, part.shape[1])] = high
        lo[:, tile(i, part.shape[1])] = low

    loop(hi.shape[1] // part.shape[1], taken)
    for copy in copies:
        copy.wait()
    finish(hi, lo, *work, in_ref, op_ref, moved_ref, out_ref)


def work_scratch(dirs, width, in_shape, op_shape):
    square = pltpu.VMEM((dirs, dirs), BF16)
    return [
        pltpu.VMEM((dirs, width), BF16),
        pltpu.VMEM((dirs, width), BF16),
        pltpu.VMEM((dirs, dirs), F32),
        square,
        square,
        pltpu.VMEM((4 * B, dirs), BF16),
        square,
        square,
        pltpu.VMEM((2 * B, width), BF16),
        pltpu.VMEM((2 * B, width), BF16),
        pltpu.VMEM((2 * B, width), BF16),
        pltpu.VMEM((2, dirs, B), F32),
        pltpu.VMEM((dirs, B), F32),
        pltpu.VMEM((B, B), F32),
        pltpu.VMEM((dirs // B, B, B), F32),
        pltpu.VMEM(in_shape, BF16),
        pltpu.VMEM(op_shape, BF16),
    ]


def ring_items(own, perms, count, cut):
    forward, backward = perms
    behind, ahead = [own], [own]
    for _ in range((count - 1) // 2):
        behind.append(lax.ppermute(behind[-1], "group", forward))
        ahead.append(lax.ppermute(ahead[-1], "group", backward))
    last = [
        lax.ppermute(behind[-1][:cut], "group", forward),
        lax.ppermute(ahead[-1][cut:], "group", backward),
    ]
    return behind + ahead[1:] + last


def per_device(acts, start_basis, out_proj, in_proj):
    tokens, width = acts[0], acts.shape[2]
    dirs = start_basis.shape[2]
    count = lax.axis_size("group")
    in_next = passed_along(in_proj[0], "section", -1)
    out_shape = (
        jax.ShapeDtypeStruct((dirs, in_next.shape[1]), BF16),
        jax.ShapeDtypeStruct((out_proj.shape[1], dirs), BF16),
    )
    scratch = work_scratch(dirs, width, in_next.shape, out_proj[0].shape)
    n_tokens = count * tokens.shape[0]
    hbm = pl.BlockSpec(memory_space=pl.ANY)
    params = pltpu.CompilerParams(vmem_limit_bytes=56 << 20)
    if count % 2 == 0 and n_tokens * width * 2 <= GATHER_LIMIT and (width // count) % B == 0:
        order = list(range(0, count, 2)) + list(range(count - 1, 0, -2))
        forward = [(order[i], order[(i + 1) % count]) for i in range(count)]
        perms = (forward, [(b, a) for a, b in forward])
        a_items = ring_items(tokens, perms, count, tokens.shape[0] // 2)
        s_items = ring_items(start_basis[0].T.astype(BF16), perms, count, dirs // 2)
        moved, rotated_out = pl.pallas_call(
            functools.partial(gathered_kernel, count),
            out_shape=out_shape,
            in_specs=[hbm] * (2 * len(a_items) + 2),
            scratch_shapes=[
                pltpu.VMEM((n_tokens, width), BF16),
                pltpu.VMEM((dirs, width), BF16),
                pltpu.VMEM((dirs, n_tokens), BF16),
            ]
            + scratch
            + [pltpu.SemaphoreType.DMA((2 * len(a_items) + 2,))],
            compiler_params=params,
        )(*a_items, *s_items, in_next, out_proj[0])
    else:
        lowered = lax.all_gather(start_basis[0].astype(BF16), "group", axis=0, tiled=True)
        projected = jnp.dot(tokens, lowered, preferred_element_type=F32).astype(BF16)
        partial = lax.dot_general(
            tokens, projected, (((0,), (0,)), ((), ())), preferred_element_type=F32
        )
        part = lax.psum_scatter(partial, "group", scatter_dimension=0, tiled=True)
        image = lax.all_gather(part, "group", axis=0, tiled=True)
        moved, rotated_out = pl.pallas_call(
            image_kernel,
            out_shape=out_shape,
            in_specs=[hbm] * 3,
            scratch_shapes=[pltpu.VMEM((dirs, 256), F32)]
            + scratch
            + [pltpu.SemaphoreType.DMA((3,))],
            compiler_params=params,
        )(image.T, in_next, out_proj[0])
    rotated_in = passed_along(moved, "section", 1)
    return (rotated_out[None], rotated_in[None])


def solution(mesh):
    in_specs = (
        P("section", "group", None),
        P("section", "group", None),
        P("section", "group", None),
        P("section", None, "group"),
    )
    out_specs = (P("section", "group", None), P("section", None, "group"))
    return jax.shard_map(
        per_device, mesh=mesh, in_specs=in_specs, out_specs=out_specs, check_vma=False
    )
```

```python
import functools

import jax
import jax.numpy as jnp
from jax import lax
from jax.experimental import pallas as pl
from jax.experimental.pallas import tpu as pltpu
from jax.sharding import PartitionSpec as P

B = 128
F32, BF16 = jnp.float32, jnp.bfloat16
HIGH = lax.Precision.HIGHEST
GATHER_LIMIT = 16 << 20
VMEM_BYTES = 48 << 20


def passed_along(value, axis, steps):
    count = lax.axis_size(axis)
    pairs = [(source, (source + steps) % count) for source in range(count)]
    return lax.ppermute(value, axis, pairs)


def nn(a, b, **kw):
    return lax.dot_general(a, b, (((1,), (0,)), ((), ())), preferred_element_type=F32, **kw)


def nt(a, b, **kw):
    return lax.dot_general(a, b, (((1,), (1,)), ((), ())), preferred_element_type=F32, **kw)


def lane_of(x, j):
    return jnp.take_along_axis(x, jnp.full((8, B), j, jnp.int32), axis=1)


def row_of(x, s):
    return jnp.broadcast_to(x[s : s + 1, :], (8, B))


def factor_core(V):
    n = len(V)
    sub = lax.broadcasted_iota(jnp.int32, (8, B), 0)
    lane = lax.broadcasted_iota(jnp.int32, (8, B), 1)
    out = []
    for p in range(n):
        in_panel = (lane >= 8 * p) & (lane < 8 * p + 8)
        C = [lane_of(V[p], 8 * p + j) for j in range(8)]
        below = {i: [lane_of(V[i], 8 * p + j) for j in range(8)] for i in range(p + 1, n)}
        X = jnp.where(in_panel, (lane - 8 * p == sub).astype(F32), V[p])
        U = X
        pivots = jnp.ones((8, B), F32)
        d = row_of(C[0], 0)
        for j in range(8):
            inv = 1.0 / d
            pivots = jnp.where(sub == j, d, pivots)
            own, pivot_column = sub == j, C[j]
            if j < 7:
                d = row_of(C[j + 1], j + 1) - (row_of(C[j], j + 1) * row_of(C[j + 1], j)) * inv
            for k in range(j + 1, 8):
                s = row_of(C[k], j) * inv
                C[k] = jnp.where(own, s, C[k] - pivot_column * s)
            x = row_of(X, j) * inv
            X = jnp.where(own, x, X - pivot_column * x)
            if j < 7:
                U = U - jnp.where(sub > j, pivot_column * inv, 0.0) * row_of(U, j)
        row = sub + 8 * p
        out.append(jnp.where(lane <= row, U * lax.rsqrt(pivots), 0.0))
        for i in range(p + 1, n):
            t = [below[i][j] * row_of(X, j) for j in range(8)]
            V[i] = jnp.where(in_panel, 0.0, V[i]) - (
                ((t[0] + t[1]) + (t[2] + t[3])) + ((t[4] + t[5]) + (t[6] + t[7]))
            )
    return out


def split(x):
    hi = x.astype(BF16)
    return hi, (x - hi.astype(F32)).astype(BF16)


def loop(count, body):
    lax.fori_loop(0, count, lambda i, c: (body(i), c)[1], 0)


def tile(i, size):
    start = i * size
    return pl.ds(start if isinstance(start, int) else pl.multiple_of(start, size), size)


def three(dot, a, b):
    return dot(a[0], b[0]) + dot(a[0], b[1]) + dot(a[1], b[0])


def factor_block(diag, w):
    for i, row in enumerate(factor_core([diag[8 * i : 8 * i + 8, :] for i in range(B // 8)])):
        w[8 * i : 8 * i + 8, :] = row


def stacked(pair, high, low):
    size = pair.shape[0] // 2
    both = nn(pair, high)
    return both[:size] + both[size:] + nn(pair[:size], low)


def finish(hi, lo, gram, lhi, llo, ecat, whi, wlo, yhi, ylo, cols, base, diag, wd, outs, in_ref, op_ref, moved_ref, out_any, fb, sem):
    dirs, width = hi.shape
    n, size = dirs // B, 2 * B
    lanes = range(0, width, size)

    def gram_tile(c):
        a, b = hi[c : c + size, :], lo[c : c + size, :]
        gram[c:, c : c + size] = nt(hi[c:, :], a) + nt(hi[c:, :], b) + nt(lo[c:, :], a)

    gram_tile(0)
    for ref in (lhi, llo, whi, wlo):
        ref[...] = jnp.zeros(ref.shape, ref.dtype)
    cols[0] = gram[:, :B]
    base[...] = gram[:, B:size]
    diag[...] = gram[:B, :B]
    row = lax.broadcasted_iota(jnp.int32, (dirs, B), 0)

    def prepare(c):
        mine = tile(c, size)
        high, rest = split(three(nn, (lhi[mine, :], llo[mine, :]), (whi[...], wlo[...])))
        ecat[:size, :] = high
        ecat[size:, :] = rest
        for d in lanes:
            at = slice(d, d + size)
            y = hi[mine, at].astype(F32) + lo[mine, at].astype(F32)
            yhi[:, at], ylo[:, at] = split(y - stacked(ecat[...], hi[:, at], lo[:, at]))

    def results(c, more):
        mine = tile(c, size)
        first, second = tile(2 * c, B), tile(2 * c + 1, B)
        wa, wb = split(wd[2 * c]), split(wd[2 * c + 1])
        between = three(nn, (lhi[second, first], llo[second, first]), wa)
        wab = -three(nn, wb, split(between))
        top = jnp.concatenate([wd[2 * c], jnp.zeros((B, B), F32)], axis=1)
        inv = split(jnp.concatenate([top, jnp.concatenate([wab, wd[2 * c + 1]], axis=1)], axis=0))
        pair = jnp.concatenate(inv, axis=0)
        if more:
            rows = split(-three(nn, inv, (ecat[:size, :], ecat[size:, :])))
            for ref, value, own in zip((whi, wlo), rows, inv):
                ref[mine, :] = value
                ref[mine, mine] = own
        for d in lanes:
            at = slice(d, d + size)
            fb[:, at] = stacked(pair, yhi[:, at], ylo[:, at]).astype(BF16)
        moved_ref[mine, :] = nn(fb[...], in_ref[...]).astype(BF16)
        if more:
            half = op_ref.shape[0] // 2
            for r in (0, half):
                outs[c, r : r + half, :] = nt(op_ref[r : r + half, :], fb[...]).astype(BF16)

    def block(k, now, beside):
        then = 1 - now
        ahead = jnp.minimum(k + 1, n - 1)
        mine, nxt = tile(k, B), tile(ahead, B)
        if not (isinstance(k, int) and k == 0):
            last = tile(k - 1, B)
            left = three(nt, split(cols[then]), split(wd[k - 1]))
            high, rest = split(jnp.where(row >= k * B, left, 0.0))
            lhi[:, last] = high
            llo[:, last] = rest
            cols[now] = base[...] - three(nt, (high, rest), (lhi[mine, last], llo[mine, last]))
            base[...] = gram[:, nxt] - three(nt, (lhi[...], llo[...]), (lhi[nxt, :], llo[nxt, :]))
        beside()
        factor_block(diag, wd.at[k])
        part = split(three(nt, split(cols[now, nxt, :]), split(wd[k])))
        diag[...] = base[nxt, :] - three(nt, part, part)

    def other_tiles():
        for c in range(2 * size, dirs, size):
            gram_tile(c)
        ecat[...] = jnp.zeros(ecat.shape, BF16)
        yhi[...] = hi[:size, :]
        ylo[...] = lo[:size, :]

    def step(i):
        b = i + 1
        block(2 * b, 0, lambda: results(b - 1, True))
        block(2 * b + 1, 1, lambda: prepare(b))

    block(0, 0, lambda: gram_tile(size))
    block(1, 1, other_tiles)
    loop(n // 2 - 1, step)
    leaving = [
        pltpu.make_async_copy(outs.at[c], out_any.at[:, pl.ds(c * size, size)], sem.at[c])
        for c in range(n // 2 - 1)
    ]
    for copy in leaving:
        copy.start()
    results(jnp.int32(n // 2 - 1), False)
    for copy in leaving:
        copy.wait()


def last_kernel(fb, op, _, out_any, out, sem):
    half = op.shape[0] // 2
    for r in (0, half):
        out[r : r + half, :] = nt(op[r : r + half, :], fb[...]).astype(BF16)
    at = pl.ds(out_any.shape[1] - out.shape[1], out.shape[1])
    copy = pltpu.make_async_copy(out, out_any.at[:, at], sem)
    copy.start()
    copy.wait()


def item_copies(count, a_items, s_items, acts, start, sems):
    full = (count - 1) // 2
    dirs, width = start.shape
    rows, cols = a_items[0].shape[0], width // count
    me = lax.axis_index("group")
    pos = jnp.where(me % 2 == 0, me // 2, count - 1 - me // 2)
    a_copies, s_copies = [], []
    for n in range(len(s_items)):
        if n < 2 * full + 1:
            step, slot, half, parts = (-n if n <= full else n - full), n, 0, 1
        else:
            step, slot, half, parts = count // 2, count - 1, n - (2 * full + 1), 2
        at = lax.rem(pos + step + count, count)
        owner = jnp.where(at < count // 2, 2 * at, 2 * (count - 1 - at) + 1)
        lanes = pl.ds(pl.multiple_of(owner * cols, cols), cols)
        if n < len(a_items):
            size = rows // parts
            to = acts.at[pl.ds(slot * rows + half * size, size), :]
            a_copies.append(pltpu.make_async_copy(a_items[n], to, sems.at[2 * n]))
        size = dirs // parts
        to = start.at[pl.ds(half * size, size), lanes]
        s_copies.append(pltpu.make_async_copy(s_items[n], to, sems.at[2 * n + 1]))
    return a_copies, s_copies


def early_kernel(count, *refs):
    full = (count - 1) // 2
    a_items, s_items = refs[: 2 * full + 1], refs[2 * full + 1 : 4 * full + 4]
    proj, acts, start, sems = refs[4 * full + 4 :]
    a_copies, s_copies = item_copies(count, a_items, s_items, acts, start, sems)
    for copy in s_copies + a_copies:
        copy.start()
    for copy in s_copies:
        copy.wait()
    rows = a_items[0].shape[0]
    for n in range(2 * full + 1):
        a_copies[n].wait()
        if n % 2 or n == 2 * full:
            at = slice((n - n % 2) * rows if n % 2 == 0 else (n - 1) * rows, (n + 1) * rows)
            proj[:, at] = nt(start[...], acts[at, :]).astype(BF16)


def gathered_kernel(count, *refs):
    n_items = 2 * ((count - 1) // 2) + 3
    a_items, s_items = refs[:n_items], refs[n_items : 2 * n_items]
    part, in_any, op_any, moved_ref, out_any, fb = refs[2 * n_items : 2 * n_items + 6]
    acts, start, proj, hi, lo, *work, in_ref, op_ref, sems, sem = refs[2 * n_items + 6 :]
    a_copies, s_copies = item_copies(count, a_items, s_items, acts, start, sems)
    known = part.shape[1]
    last = 2 * n_items
    others = [
        pltpu.make_async_copy(part, proj.at[:, pl.ds(0, known)], sems.at[last]),
        pltpu.make_async_copy(in_any, in_ref, sems.at[last + 1]),
        pltpu.make_async_copy(op_any, op_ref, sems.at[last + 2]),
    ]
    order = s_copies + a_copies[-2:] + others[:1] + a_copies[:-2] + others[1:]
    for copy in order:
        copy.start()
    for copy in s_copies + a_copies[-2:]:
        copy.wait()
    proj[:, known:] = nt(start[...], acts[known:, :]).astype(BF16)
    for copy in others[:1] + a_copies[:-2]:
        copy.wait()
    size = 2 * B
    for i in range(hi.shape[1] // size):
        at = tile(i, size)
        hi[:, at], lo[:, at] = split(nn(proj[...], acts[:, at]))
    for copy in others[1:]:
        copy.wait()
    finish(hi, lo, *work, in_ref, op_ref, moved_ref, out_any, fb, sem)


def image_kernel(image_any, in_any, op_any, moved_ref, out_any, fb, part, hi, lo, *rest):
    *work, in_ref, op_ref, sems, sem = rest
    copies = [
        pltpu.make_async_copy(in_any, in_ref, sems.at[0]),
        pltpu.make_async_copy(op_any, op_ref, sems.at[1]),
    ]
    for copy in copies:
        copy.start()

    def taken(i):
        c = pltpu.make_async_copy(image_any.at[:, tile(i, part.shape[1])], part, sems.at[2])
        c.start()
        c.wait()
        high, low = split(part[...])
        hi[:, tile(i, part.shape[1])] = high
        lo[:, tile(i, part.shape[1])] = low

    loop(hi.shape[1] // part.shape[1], taken)
    for copy in copies:
        copy.wait()
    finish(hi, lo, *work, in_ref, op_ref, moved_ref, out_any, fb, sem)


def work_scratch(dirs, width, in_shape, op_shape):
    square = pltpu.VMEM((dirs, dirs), BF16)
    return [
        pltpu.VMEM((dirs, width), BF16),
        pltpu.VMEM((dirs, width), BF16),
        pltpu.VMEM((dirs, dirs), F32),
        square,
        square,
        pltpu.VMEM((4 * B, dirs), BF16),
        square,
        square,
        pltpu.VMEM((2 * B, width), BF16),
        pltpu.VMEM((2 * B, width), BF16),
        pltpu.VMEM((2, dirs, B), F32),
        pltpu.VMEM((dirs, B), F32),
        pltpu.VMEM((B, B), F32),
        pltpu.VMEM((dirs // B, B, B), F32),
        pltpu.VMEM((dirs // (2 * B) - 1, op_shape[0], 2 * B), BF16),
        pltpu.VMEM(in_shape, BF16),
        pltpu.VMEM(op_shape, BF16),
    ]


def ring_items(own, perms, count, cut):
    forward, backward = perms
    behind, ahead = [own], [own]
    for _ in range((count - 1) // 2):
        behind.append(lax.ppermute(behind[-1], "group", forward))
        ahead.append(lax.ppermute(ahead[-1], "group", backward))
    last = [
        lax.ppermute(behind[-1][:cut], "group", forward),
        lax.ppermute(ahead[-1][cut:], "group", backward),
    ]
    return behind + ahead[1:] + last


def per_device(acts, start_basis, out_proj, in_proj):
    tokens, width = acts[0], acts.shape[2]
    dirs = start_basis.shape[2]
    count = lax.axis_size("group")
    in_next = passed_along(in_proj[0], "section", -1)
    out_shape = (
        jax.ShapeDtypeStruct((dirs, in_next.shape[1]), BF16),
        jax.ShapeDtypeStruct((out_proj.shape[1], dirs), BF16),
        jax.ShapeDtypeStruct((2 * B, width), BF16),
    )
    scratch = work_scratch(dirs, width, in_next.shape, out_proj[0].shape)
    leaving = pltpu.SemaphoreType.DMA((dirs // (2 * B) - 1,))
    n_tokens = count * tokens.shape[0]
    hbm, vmem = pl.BlockSpec(memory_space=pl.ANY), pl.BlockSpec(memory_space=pltpu.VMEM)
    params = pltpu.CompilerParams(vmem_limit_bytes=VMEM_BYTES)
    if count % 2 == 0 and n_tokens * width * 2 <= GATHER_LIMIT and (width // count) % B == 0:
        order = list(range(0, count, 2)) + list(range(count - 1, 0, -2))
        forward = [(order[i], order[(i + 1) % count]) for i in range(count)]
        perms = (forward, [(b, a) for a, b in forward])
        s_items = ring_items(start_basis[0].T.astype(BF16), perms, count, dirs // 2)
        a_items = ring_items(tokens, perms, count, tokens.shape[0] // 2)
        known = n_tokens - tokens.shape[0]
        gathered = [pltpu.VMEM((n_tokens, width), BF16), pltpu.VMEM((dirs, width), BF16)]
        sems = pltpu.SemaphoreType.DMA((2 * len(a_items) + 3,))
        part = pl.pallas_call(
            functools.partial(early_kernel, count),
            out_shape=jax.ShapeDtypeStruct((dirs, known), BF16),
            in_specs=[hbm] * (2 * len(a_items) - 2),
            out_specs=vmem,
            scratch_shapes=[*gathered, sems],
            compiler_params=pltpu.CompilerParams(vmem_limit_bytes=VMEM_BYTES // 2),
            cost_estimate=pl.CostEstimate(
                flops=2 * dirs * width * known, bytes_accessed=10 << 20, transcendentals=0
            ),
        )(*a_items[:-2], *s_items)
        moved, rotated, final = pl.pallas_call(
            functools.partial(gathered_kernel, count),
            out_shape=out_shape,
            in_specs=[hbm] * (2 * len(a_items) + 3),
            out_specs=(vmem, hbm, vmem),
            scratch_shapes=[*gathered, pltpu.VMEM((dirs, n_tokens), BF16), *scratch, sems, leaving],
            compiler_params=params,
        )(*a_items, *s_items, part, in_next, out_proj[0])
    else:
        lowered = lax.all_gather(start_basis[0].astype(BF16), "group", axis=0, tiled=True)
        projected = jnp.dot(tokens, lowered, preferred_element_type=F32).astype(BF16)
        partial = lax.dot_general(
            tokens, projected, (((0,), (0,)), ((), ())), preferred_element_type=F32
        )
        part = lax.psum_scatter(partial, "group", scatter_dimension=0, tiled=True)
        image = lax.all_gather(part, "group", axis=0, tiled=True)
        moved, rotated, final = pl.pallas_call(
            image_kernel,
            out_shape=out_shape,
            in_specs=[hbm] * 3,
            out_specs=(vmem, hbm, vmem),
            scratch_shapes=[
                pltpu.VMEM((dirs, 256), F32),
                *scratch,
                pltpu.SemaphoreType.DMA((3,)),
                leaving,
            ],
            compiler_params=params,
        )(image.T, in_next, out_proj[0])
    rotated_in = passed_along(moved, "section", 1)
    rotated_out = pl.pallas_call(
        last_kernel,
        out_shape=out_shape[1],
        in_specs=[vmem, vmem, hbm],
        out_specs=hbm,
        scratch_shapes=[
            pltpu.VMEM((out_proj.shape[1], 2 * B), BF16),
            pltpu.SemaphoreType.DMA,
        ],
        input_output_aliases={2: 0},
        compiler_params=pltpu.CompilerParams(vmem_limit_bytes=12 << 20),
        cost_estimate=pl.CostEstimate(
            flops=4 * B * width * out_proj.shape[1], bytes_accessed=6 << 20, transcendentals=0
        ),
    )(final, out_proj[0], rotated)
    return (rotated_out[None], rotated_in[None])


def solution(mesh):
    in_specs = (
        P("section", "group", None),
        P("section", "group", None),
        P("section", "group", None),
        P("section", None, "group"),
    )
    out_specs = (P("section", "group", None), P("section", None, "group"))
    return jax.shard_map(
        per_device, mesh=mesh, in_specs=in_specs, out_specs=out_specs, check_vma=False
    )
```

```python
import functools

import jax
import jax.numpy as jnp
from jax import lax
from jax.experimental import pallas as pl
from jax.experimental.pallas import tpu as pltpu
from jax.sharding import PartitionSpec as P

B = 128
F32, BF16 = jnp.float32, jnp.bfloat16
HIGH = lax.Precision.HIGHEST
GATHER_LIMIT = 16 << 20
VMEM_BYTES = 58 << 20


def passed_along(value, axis, steps):
    count = lax.axis_size(axis)
    pairs = [(source, (source + steps) % count) for source in range(count)]
    return lax.ppermute(value, axis, pairs)


def nn(a, b, **kw):
    return lax.dot_general(a, b, (((1,), (0,)), ((), ())), preferred_element_type=F32, **kw)


def nt(a, b, **kw):
    return lax.dot_general(a, b, (((1,), (1,)), ((), ())), preferred_element_type=F32, **kw)


def lane_of(x, j):
    return jnp.take_along_axis(x, jnp.full((8, B), j, jnp.int32), axis=1)


def row_of(x, s):
    return jnp.broadcast_to(x[s : s + 1, :], (8, B))


def factor_core(V):
    n = len(V)
    sub = lax.broadcasted_iota(jnp.int32, (8, B), 0)
    lane = lax.broadcasted_iota(jnp.int32, (8, B), 1)
    out = []
    for p in range(n):
        in_panel = (lane >= 8 * p) & (lane < 8 * p + 8)
        C = [lane_of(V[p], 8 * p + j) for j in range(8)]
        below = {i: [lane_of(V[i], 8 * p + j) for j in range(8)] for i in range(p + 1, n)}
        X = jnp.where(in_panel, (lane - 8 * p == sub).astype(F32), V[p])
        U = X
        pivots = jnp.ones((8, B), F32)
        d = row_of(C[0], 0)
        for j in range(8):
            inv = 1.0 / d
            pivots = jnp.where(sub == j, d, pivots)
            own, pivot_column = sub == j, C[j]
            if j < 7:
                d = row_of(C[j + 1], j + 1) - (row_of(C[j], j + 1) * row_of(C[j + 1], j)) * inv
            for k in range(j + 1, 8):
                s = row_of(C[k], j) * inv
                C[k] = jnp.where(own, s, C[k] - pivot_column * s)
            x = row_of(X, j) * inv
            X = jnp.where(own, x, X - pivot_column * x)
            if j < 7:
                U = U - jnp.where(sub > j, pivot_column * inv, 0.0) * row_of(U, j)
        row = sub + 8 * p
        out.append(jnp.where(lane <= row, U * lax.rsqrt(pivots), 0.0))
        for i in range(p + 1, n):
            t = [below[i][j] * row_of(X, j) for j in range(8)]
            V[i] = jnp.where(in_panel, 0.0, V[i]) - (
                ((t[0] + t[1]) + (t[2] + t[3])) + ((t[4] + t[5]) + (t[6] + t[7]))
            )
    return out


def split(x):
    hi = x.astype(BF16)
    return hi, (x - hi.astype(F32)).astype(BF16)


def loop(count, body):
    lax.fori_loop(0, count, lambda i, c: (body(i), c)[1], 0)


def tile(i, size):
    start = i * size
    return pl.ds(start if isinstance(start, int) else pl.multiple_of(start, size), size)


def three(dot, a, b):
    return dot(a[0], b[0]) + dot(a[0], b[1]) + dot(a[1], b[0])


def factor_block(diag, w):
    for i, row in enumerate(factor_core([diag[8 * i : 8 * i + 8, :] for i in range(B // 8)])):
        w[8 * i : 8 * i + 8, :] = row


def stacked(pair, high, low):
    size = pair.shape[0] // 2
    both = nn(pair, high)
    return both[:size] + both[size:] + nn(pair[:size], low)


def finish(hi, lo, gram, lhi, llo, ecat, whi, wlo, yhi, ylo, cols, base, diag, wd, outs, in_ref, op_ref, moved_ref, out_any, fb, sem):
    dirs, width = hi.shape
    n, size = dirs // B, 2 * B
    lanes = range(0, width, size)

    def gram_tile(c):
        a, b = hi[c : c + size, :], lo[c : c + size, :]
        gram[c:, c : c + size] = nt(hi[c:, :], a) + nt(hi[c:, :], b) + nt(lo[c:, :], a)

    gram_tile(0)
    for ref in (whi, wlo):
        ref[...] = jnp.zeros(ref.shape, ref.dtype)
    cols[0] = gram[:, :B]
    base[...] = gram[:, B:size]
    diag[...] = gram[:B, :B]

    def prepare(c):
        m = c * size
        mine = slice(m, m + size)
        if m:
            left = lhi[mine, :m], llo[mine, :m]
            high, rest = split(three(nn, left, (whi[:m, :m], wlo[:m, :m])))
            ecat[:size, :m] = high
            ecat[size:, :m] = rest
        for d in lanes:
            at = slice(d, d + size)
            if m:
                y = hi[mine, at].astype(F32) + lo[mine, at].astype(F32)
                y = y - stacked(ecat[:, :m], hi[:m, at], lo[:m, at])
                yhi[:, at], ylo[:, at] = split(y)
            else:
                yhi[:, at], ylo[:, at] = hi[mine, at], lo[mine, at]

    def results(c):
        m = c * size
        mine = slice(m, m + size)
        first, second = slice(m, m + B), slice(m + B, m + size)
        wa, wb = split(wd[2 * c]), split(wd[2 * c + 1])
        between = three(nn, (lhi[second, first], llo[second, first]), wa)
        wab = -three(nn, wb, split(between))
        top = jnp.concatenate([wd[2 * c], jnp.zeros((B, B), F32)], axis=1)
        inv = split(jnp.concatenate([top, jnp.concatenate([wab, wd[2 * c + 1]], axis=1)], axis=0))
        pair = jnp.concatenate(inv, axis=0)
        more = m + size < dirs
        if more:
            whi[mine, mine], wlo[mine, mine] = inv
            if m:
                below = -three(nn, inv, (ecat[:size, :m], ecat[size:, :m]))
                whi[mine, :m], wlo[mine, :m] = split(below)
        for d in lanes:
            at = slice(d, d + size)
            fb[:, at] = stacked(pair, yhi[:, at], ylo[:, at]).astype(BF16)
        moved_ref[mine, :] = nn(fb[...], in_ref[...]).astype(BF16)
        if more:
            half = op_ref.shape[0] // 2
            for r in (0, half):
                outs[c, r : r + half, :] = nt(op_ref[r : r + half, :], fb[...]).astype(BF16)

    def block(k, beside):
        now, then = k % 2, 1 - k % 2
        r, q = k * B, (k + 1) * B
        if k:
            pair = split(three(nt, split(cols[then, r:, :]), split(wd[k - 1])))
            lhi[r:, r - B : r], llo[r:, r - B : r] = pair
            cols[now, r:, :] = base[r:, :] - three(nt, pair, (pair[0][:B], pair[1][:B]))
            if q < dirs:
                base[q:, :] = gram[q:, q : q + B] - three(
                    nt, (lhi[q:, :r], llo[q:, :r]), (lhi[q : q + B, :r], llo[q : q + B, :r])
                )
        beside()
        factor_block(diag, wd.at[k])
        if q < dirs:
            part = split(three(nt, split(cols[now, q : q + B, :]), split(wd[k])))
            diag[...] = base[q : q + B, :] - three(nt, part, part)

    def other_tiles():
        for c in range(2 * size, dirs, size):
            gram_tile(c)
        prepare(0)

    block(0, lambda: gram_tile(size))
    block(1, other_tiles)
    for b in range(1, n // 2):
        block(2 * b, lambda: results(b - 1))
        block(2 * b + 1, lambda: prepare(b))
    leaving = [
        pltpu.make_async_copy(outs.at[c], out_any.at[:, pl.ds(c * size, size)], sem.at[c])
        for c in range(n // 2 - 1)
    ]
    for copy in leaving:
        copy.start()
    results(n // 2 - 1)
    for copy in leaving:
        copy.wait()


def last_kernel(pieces, fb, op_any, _, out_any, op, out, sems):
    rows, width = op.shape[0] // pieces, out.shape[1]
    at = pl.ds(out_any.shape[1] - width, width)
    each = [pl.ds(i * rows, rows) for i in range(pieces)]
    come = [pltpu.make_async_copy(op_any.at[r, :], op.at[r, :], sems.at[i]) for i, r in enumerate(each)]
    go = [
        pltpu.make_async_copy(out.at[r, :], out_any.at[r, at], sems.at[pieces + i])
        for i, r in enumerate(each)
    ]
    for copy in come:
        copy.start()
    for i in range(pieces):
        come[i].wait()
        out[each[i], :] = nt(op[each[i], :], fb[...]).astype(BF16)
        go[i].start()
    for copy in go:
        copy.wait()


def item_copies(count, a_items, s_items, acts, start, sems):
    full = (count - 1) // 2
    dirs, width = start.shape
    rows, cols = a_items[0].shape[0], width // count
    me = lax.axis_index("group")
    pos = jnp.where(me % 2 == 0, me // 2, count - 1 - me // 2)
    a_copies, s_copies = [], []
    for n in range(len(s_items)):
        if n < 2 * full + 1:
            step, slot, half, parts = (-n if n <= full else n - full), n, 0, 1
        else:
            step, slot, half, parts = count // 2, count - 1, n - (2 * full + 1), 2
        at = lax.rem(pos + step + count, count)
        owner = jnp.where(at < count // 2, 2 * at, 2 * (count - 1 - at) + 1)
        lanes = pl.ds(pl.multiple_of(owner * cols, cols), cols)
        if n < len(a_items):
            size = rows // parts
            to = acts.at[pl.ds(slot * rows + half * size, size), :]
            a_copies.append(pltpu.make_async_copy(a_items[n], to, sems.at[2 * n]))
        size = dirs // parts
        to = start.at[pl.ds(half * size, size), lanes]
        s_copies.append(pltpu.make_async_copy(s_items[n], to, sems.at[2 * n + 1]))
    return a_copies, s_copies


def gathered_kernel(count, *refs):
    n_items = 2 * ((count - 1) // 2) + 3
    a_items, s_items = refs[:n_items], refs[n_items : 2 * n_items]
    in_any, op_any, moved_ref, out_any, fb = refs[2 * n_items : 2 * n_items + 5]
    acts, start, proj, hi, lo, *work, in_ref, op_ref, sems, sem = refs[2 * n_items + 5 :]
    a_copies, s_copies = item_copies(count, a_items, s_items, acts, start, sems)
    others = [
        pltpu.make_async_copy(in_any, in_ref, sems.at[2 * n_items]),
        pltpu.make_async_copy(op_any, op_ref, sems.at[2 * n_items + 1]),
    ]
    for copy in s_copies + a_copies + others:
        copy.start()
    for copy in s_copies:
        copy.wait()
    rows, size = a_items[0].shape[0], 2 * B
    for n in range(0, count, 2):
        for copy in a_copies[n : n + 2] if n + 2 < count else a_copies[n:]:
            copy.wait()
        at = slice(n * rows, (n + 2) * rows)
        proj[:, at] = nt(start[...], acts[at, :]).astype(BF16)
    for i in range(hi.shape[1] // size):
        at = tile(i, size)
        hi[:, at], lo[:, at] = split(nn(proj[...], acts[:, at]))
    for copy in others:
        copy.wait()
    finish(hi, lo, *work, in_ref, op_ref, moved_ref, out_any, fb, sem)


def image_kernel(image_any, in_any, op_any, moved_ref, out_any, fb, part, hi, lo, *rest):
    *work, in_ref, op_ref, sems, sem = rest
    copies = [
        pltpu.make_async_copy(in_any, in_ref, sems.at[0]),
        pltpu.make_async_copy(op_any, op_ref, sems.at[1]),
    ]
    for copy in copies:
        copy.start()

    def taken(i):
        c = pltpu.make_async_copy(image_any.at[:, tile(i, part.shape[1])], part, sems.at[2])
        c.start()
        c.wait()
        high, low = split(part[...])
        hi[:, tile(i, part.shape[1])] = high
        lo[:, tile(i, part.shape[1])] = low

    loop(hi.shape[1] // part.shape[1], taken)
    for copy in copies:
        copy.wait()
    finish(hi, lo, *work, in_ref, op_ref, moved_ref, out_any, fb, sem)


def work_scratch(dirs, width, in_shape, op_shape):
    square = pltpu.VMEM((dirs, dirs), BF16)
    return [
        pltpu.VMEM((dirs, width), BF16),
        pltpu.VMEM((dirs, width), BF16),
        pltpu.VMEM((dirs, dirs), F32),
        square,
        square,
        pltpu.VMEM((4 * B, dirs), BF16),
        square,
        square,
        pltpu.VMEM((2 * B, width), BF16),
        pltpu.VMEM((2 * B, width), BF16),
        pltpu.VMEM((2, dirs, B), F32),
        pltpu.VMEM((dirs, B), F32),
        pltpu.VMEM((B, B), F32),
        pltpu.VMEM((dirs // B, B, B), F32),
        pltpu.VMEM((dirs // (2 * B) - 1, op_shape[0], 2 * B), BF16),
        pltpu.VMEM(in_shape, BF16),
        pltpu.VMEM(op_shape, BF16),
    ]


def ring_items(own, perms, count, cut):
    forward, backward = perms
    behind, ahead = [own], [own]
    for _ in range((count - 1) // 2):
        behind.append(lax.ppermute(behind[-1], "group", forward))
        ahead.append(lax.ppermute(ahead[-1], "group", backward))
    last = [
        lax.ppermute(behind[-1][:cut], "group", forward),
        lax.ppermute(ahead[-1][cut:], "group", backward),
    ]
    return behind + ahead[1:] + last


def per_device(acts, start_basis, out_proj, in_proj):
    tokens, width = acts[0], acts.shape[2]
    dirs = start_basis.shape[2]
    count = lax.axis_size("group")
    in_next = passed_along(in_proj[0], "section", -1)
    out_shape = (
        jax.ShapeDtypeStruct((dirs, in_next.shape[1]), BF16),
        jax.ShapeDtypeStruct((out_proj.shape[1], dirs), BF16),
        jax.ShapeDtypeStruct((2 * B, width), BF16),
    )
    scratch = work_scratch(dirs, width, in_next.shape, out_proj[0].shape)
    leaving = pltpu.SemaphoreType.DMA((dirs // (2 * B) - 1,))
    n_tokens = count * tokens.shape[0]
    hbm, vmem = pl.BlockSpec(memory_space=pl.ANY), pl.BlockSpec(memory_space=pltpu.VMEM)
    params = pltpu.CompilerParams(vmem_limit_bytes=VMEM_BYTES)
    if count % 2 == 0 and n_tokens * width * 2 <= GATHER_LIMIT and (width // count) % B == 0:
        order = list(range(0, count, 2)) + list(range(count - 1, 0, -2))
        forward = [(order[i], order[(i + 1) % count]) for i in range(count)]
        perms = (forward, [(b, a) for a, b in forward])
        s_items = ring_items(start_basis[0].T.astype(BF16), perms, count, dirs // 2)
        a_items = ring_items(tokens, perms, count, tokens.shape[0] // 2)
        gathered = [pltpu.VMEM((n_tokens, width), BF16), pltpu.VMEM((dirs, width), BF16)]
        sems = pltpu.SemaphoreType.DMA((2 * len(a_items) + 2,))
        moved, rotated, final = pl.pallas_call(
            functools.partial(gathered_kernel, count),
            out_shape=out_shape,
            in_specs=[hbm] * (2 * len(a_items) + 2),
            out_specs=(vmem, hbm, vmem),
            scratch_shapes=[*gathered, pltpu.VMEM((dirs, n_tokens), BF16), *scratch, sems, leaving],
            compiler_params=params,
        )(*a_items, *s_items, in_next, out_proj[0])
    else:
        lowered = lax.all_gather(start_basis[0].astype(BF16), "group", axis=0, tiled=True)
        projected = jnp.dot(tokens, lowered, preferred_element_type=F32).astype(BF16)
        partial = lax.dot_general(
            tokens, projected, (((0,), (0,)), ((), ())), preferred_element_type=F32
        )
        part = lax.psum_scatter(partial, "group", scatter_dimension=0, tiled=True)
        image = lax.all_gather(part, "group", axis=0, tiled=True)
        moved, rotated, final = pl.pallas_call(
            image_kernel,
            out_shape=out_shape,
            in_specs=[hbm] * 3,
            out_specs=(vmem, hbm, vmem),
            scratch_shapes=[
                pltpu.VMEM((dirs, 256), F32),
                *scratch,
                pltpu.SemaphoreType.DMA((3,)),
                leaving,
            ],
            compiler_params=params,
        )(image.T, in_next, out_proj[0])
    rotated_in = passed_along(moved, "section", 1)
    pieces = 4 if out_proj.shape[1] % 256 == 0 else 1
    rotated_out = pl.pallas_call(
        functools.partial(last_kernel, pieces),
        out_shape=out_shape[1],
        in_specs=[vmem, hbm, hbm],
        out_specs=hbm,
        scratch_shapes=[
            pltpu.VMEM(out_proj[0].shape, BF16),
            pltpu.VMEM((out_proj.shape[1], 2 * B), BF16),
            pltpu.SemaphoreType.DMA((2 * pieces,)),
        ],
        input_output_aliases={2: 0},
        compiler_params=pltpu.CompilerParams(vmem_limit_bytes=VMEM_BYTES),
        cost_estimate=pl.CostEstimate(
            flops=4 * B * width * out_proj.shape[1], bytes_accessed=6 << 20, transcendentals=0
        ),
    )(final, out_proj[0], rotated)
    return (rotated_out[None], rotated_in[None])


def solution(mesh):
    in_specs = (
        P("section", "group", None),
        P("section", "group", None),
        P("section", "group", None),
        P("section", None, "group"),
    )
    out_specs = (P("section", "group", None), P("section", None, "group"))
    return jax.shard_map(
        per_device, mesh=mesh, in_specs=in_specs, out_specs=out_specs, check_vma=False
    )
```

```python
import functools

import jax
import jax.numpy as jnp
from jax import lax
from jax.experimental import pallas as pl
from jax.experimental.pallas import tpu as pltpu
from jax.sharding import PartitionSpec as P

B = 128
F32, BF16 = jnp.float32, jnp.bfloat16
HIGH = lax.Precision.HIGHEST
GATHER_LIMIT = 16 << 20
VMEM_BYTES = 58 << 20


def passed_along(value, axis, steps):
    count = lax.axis_size(axis)
    pairs = [(source, (source + steps) % count) for source in range(count)]
    return lax.ppermute(value, axis, pairs)


def nn(a, b, **kw):
    return lax.dot_general(a, b, (((1,), (0,)), ((), ())), preferred_element_type=F32, **kw)


def nt(a, b, **kw):
    return lax.dot_general(a, b, (((1,), (1,)), ((), ())), preferred_element_type=F32, **kw)


def lane_of(x, j):
    return jnp.take_along_axis(x, jnp.full((8, B), j, jnp.int32), axis=1)


def row_of(x, s):
    return jnp.broadcast_to(x[s : s + 1, :], (8, B))


def factor_core(V):
    n = len(V)
    sub = lax.broadcasted_iota(jnp.int32, (8, B), 0)
    lane = lax.broadcasted_iota(jnp.int32, (8, B), 1)
    out = []
    for p in range(n):
        in_panel = (lane >= 8 * p) & (lane < 8 * p + 8)
        C = [lane_of(V[p], 8 * p + j) for j in range(8)]
        below = {i: [lane_of(V[i], 8 * p + j) for j in range(8)] for i in range(p + 1, n)}
        X = jnp.where(in_panel, (lane - 8 * p == sub).astype(F32), V[p])
        U = X
        pivots = jnp.ones((8, B), F32)
        d = row_of(C[0], 0)
        for j in range(8):
            inv = 1.0 / d
            pivots = jnp.where(sub == j, d, pivots)
            own, pivot_column = sub == j, C[j]
            if j < 7:
                d = row_of(C[j + 1], j + 1) - (row_of(C[j], j + 1) * row_of(C[j + 1], j)) * inv
            for k in range(j + 1, 8):
                s = row_of(C[k], j) * inv
                C[k] = jnp.where(own, s, C[k] - pivot_column * s)
            x = row_of(X, j) * inv
            X = jnp.where(own, x, X - pivot_column * x)
            if j < 7:
                U = U - jnp.where(sub > j, pivot_column * inv, 0.0) * row_of(U, j)
        row = sub + 8 * p
        out.append(jnp.where(lane <= row, U * lax.rsqrt(pivots), 0.0))
        for i in range(p + 1, n):
            t = [below[i][j] * row_of(X, j) for j in range(8)]
            V[i] = jnp.where(in_panel, 0.0, V[i]) - (
                ((t[0] + t[1]) + (t[2] + t[3])) + ((t[4] + t[5]) + (t[6] + t[7]))
            )
    return out


def split(x):
    hi = x.astype(BF16)
    return hi, (x - hi.astype(F32)).astype(BF16)


def loop(count, body):
    lax.fori_loop(0, count, lambda i, c: (body(i), c)[1], 0)


def tile(i, size):
    start = i * size
    return pl.ds(start if isinstance(start, int) else pl.multiple_of(start, size), size)


def three(dot, a, b):
    return dot(a[0], b[0]) + dot(a[0], b[1]) + dot(a[1], b[0])


def factor_block(diag, w):
    for i, row in enumerate(factor_core([diag[8 * i : 8 * i + 8, :] for i in range(B // 8)])):
        w[8 * i : 8 * i + 8, :] = row


def stacked(pair, high, low):
    size = pair.shape[0] // 2
    both = nn(pair, high)
    return both[:size] + both[size:] + nn(pair[:size], low)


def finish(hi, lo, gram, lhi, llo, ecat, whi, wlo, yhi, ylo, cols, base, diag, wd, outs, in_ref, op_ref, moved_ref, out_any, fb, sem, rest):
    dirs, width = hi.shape
    n, size = dirs // B, 2 * B
    lanes = range(0, width, size)

    def gram_part(r, end, c):
        a, b = hi[c : c + size, :], lo[c : c + size, :]
        x, y = hi[r:end, :], lo[r:end, :]
        gram[r:end, c : c + size] = nt(x, a) + nt(x, b) + nt(y, a)

    def first_columns(r, end):
        gram_part(r, end, 0)
        cols[0, r:end, :] = gram[r:end, :B]
        base[r:end, :] = gram[r:end, B:size]

    first_columns(0, size)
    for ref in (whi, wlo):
        ref[...] = jnp.zeros(ref.shape, ref.dtype)
    diag[...] = gram[:B, :B]

    def prepare(c):
        m = c * size
        mine = slice(m, m + size)
        if m:
            left = lhi[mine, :m], llo[mine, :m]
            high, rest = split(three(nn, left, (whi[:m, :m], wlo[:m, :m])))
            ecat[:size, :m] = high
            ecat[size:, :m] = rest
        for d in lanes:
            at = slice(d, d + size)
            if m:
                y = hi[mine, at].astype(F32) + lo[mine, at].astype(F32)
                y = y - stacked(ecat[:, :m], hi[:m, at], lo[:m, at])
                yhi[:, at], ylo[:, at] = split(y)
            else:
                yhi[:, at], ylo[:, at] = hi[mine, at], lo[mine, at]

    def results(c):
        m = c * size
        mine = slice(m, m + size)
        first, second = slice(m, m + B), slice(m + B, m + size)
        wa, wb = split(wd[2 * c]), split(wd[2 * c + 1])
        between = three(nn, (lhi[second, first], llo[second, first]), wa)
        wab = -three(nn, wb, split(between))
        top = jnp.concatenate([wd[2 * c], jnp.zeros((B, B), F32)], axis=1)
        inv = split(jnp.concatenate([top, jnp.concatenate([wab, wd[2 * c + 1]], axis=1)], axis=0))
        pair = jnp.concatenate(inv, axis=0)
        more = m + size < dirs
        if more:
            whi[mine, mine], wlo[mine, mine] = inv
            if m:
                below = -three(nn, inv, (ecat[:size, :m], ecat[size:, :m]))
                whi[mine, :m], wlo[mine, :m] = split(below)
        for d in lanes:
            at = slice(d, d + size)
            fb[:, at] = stacked(pair, yhi[:, at], ylo[:, at]).astype(BF16)
        moved_ref[mine, :] = nn(fb[...], in_ref[...]).astype(BF16)
        if more:
            half = op_ref.shape[0] // 2
            for r in (0, half):
                outs[c, r : r + half, :] = nt(op_ref[r : r + half, :], fb[...]).astype(BF16)

    def update(k, first, end):
        r, then = k * B, 1 - k % 2
        pair = split(three(nt, split(cols[then, first:end, :]), split(wd[k - 1])))
        lhi[first:end, r - B : r], llo[first:end, r - B : r] = pair
        mine = lhi[r : r + B, r - B : r], llo[r : r + B, r - B : r]
        cols[k % 2, first:end, :] = base[first:end, :] - three(nt, pair, mine)

    def next_base(k):
        r, q = k * B, (k + 1) * B
        taken = (lhi[q:, :r], llo[q:, :r]), (lhi[q : q + B, :r], llo[q : q + B, :r])
        base[q:, :] = gram[q:, q : q + B] - three(nt, *taken)

    def block(k, beside):
        q = (k + 1) * B
        if k == 1:
            update(k, B, size)
        elif k:
            update(k, k * B, dirs)
            if q < dirs:
                next_base(k)
        beside()
        factor_block(diag, wd.at[k])
        if q < dirs:
            part = split(three(nt, split(cols[k % 2, q : q + B, :]), split(wd[k])))
            diag[...] = base[q : q + B, :] - three(nt, part, part)

    def late():
        if size < dirs:
            first_columns(size, dirs)
            update(1, size, dirs)
            for c in range(size, dirs, size):
                gram_part(c, dirs, c)
            next_base(1)
        prepare(0)

    block(0, rest)
    block(1, late)
    for b in range(1, n // 2):
        block(2 * b, lambda: results(b - 1))
        block(2 * b + 1, lambda: prepare(b))
    leaving = [
        pltpu.make_async_copy(outs.at[c], out_any.at[:, pl.ds(c * size, size)], sem.at[c])
        for c in range(n // 2 - 1)
    ]
    for copy in leaving:
        copy.start()
    results(n // 2 - 1)
    for copy in leaving:
        copy.wait()


def last_kernel(pieces, fb, op_any, _, out_any, op, out, sems):
    rows, width = op.shape[0] // pieces, out.shape[1]
    at = pl.ds(out_any.shape[1] - width, width)
    each = [pl.ds(i * rows, rows) for i in range(pieces)]
    come = [pltpu.make_async_copy(op_any.at[r, :], op.at[r, :], sems.at[i]) for i, r in enumerate(each)]
    go = [
        pltpu.make_async_copy(out.at[r, :], out_any.at[r, at], sems.at[pieces + i])
        for i, r in enumerate(each)
    ]
    for copy in come:
        copy.start()
    for i in range(pieces):
        come[i].wait()
        out[each[i], :] = nt(op[each[i], :], fb[...]).astype(BF16)
        go[i].start()
    for copy in go:
        copy.wait()


def item_copies(count, a_items, s_items, acts, start, sems):
    full = (count - 1) // 2
    dirs, width = start.shape
    rows, cols = a_items[0].shape[0], width // count
    me = lax.axis_index("group")
    pos = jnp.where(me % 2 == 0, me // 2, count - 1 - me // 2)
    a_copies, s_copies = [], []
    for n in range(len(s_items)):
        if n < 2 * full + 1:
            step, slot, half, parts = (-n if n <= full else n - full), n, 0, 1
        else:
            step, slot, half, parts = count // 2, count - 1, n - (2 * full + 1), 2
        at = lax.rem(pos + step + count, count)
        owner = jnp.where(at < count // 2, 2 * at, 2 * (count - 1 - at) + 1)
        lanes = pl.ds(pl.multiple_of(owner * cols, cols), cols)
        if n < len(a_items):
            size = rows // parts
            to = acts.at[pl.ds(slot * rows + half * size, size), :]
            a_copies.append(pltpu.make_async_copy(a_items[n], to, sems.at[2 * n]))
        size = dirs // parts
        to = start.at[pl.ds(half * size, size), lanes]
        s_copies.append(pltpu.make_async_copy(s_items[n], to, sems.at[2 * n + 1]))
    return a_copies, s_copies


def gathered_kernel(count, *refs):
    n_items = 2 * ((count - 1) // 2) + 3
    a_items, s_items = refs[:n_items], refs[n_items : 2 * n_items]
    in_any, op_any, moved_ref, out_any, fb = refs[2 * n_items : 2 * n_items + 5]
    acts, start, proj, hi, lo, *work, in_ref, op_ref, sems, sem = refs[2 * n_items + 5 :]
    a_copies, s_copies = item_copies(count, a_items, s_items, acts, start, sems)
    others = [
        pltpu.make_async_copy(in_any, in_ref, sems.at[2 * n_items]),
        pltpu.make_async_copy(op_any, op_ref, sems.at[2 * n_items + 1]),
    ]
    for copy in s_copies + a_copies + others:
        copy.start()
    for copy in s_copies:
        copy.wait()
    rows, size = a_items[0].shape[0], 2 * B
    for n in range(0, count, 2):
        for copy in a_copies[n : n + 2] if n + 2 < count else a_copies[n:]:
            copy.wait()
        at = slice(n * rows, (n + 2) * rows)
        proj[:size, at] = nt(start[:size, :], acts[at, :]).astype(BF16)

    def cover(r, end):
        for d in range(0, hi.shape[1], size):
            at = slice(d, d + size)
            hi[r:end, at], lo[r:end, at] = split(nn(proj[r:end, :], acts[:, at]))

    def rest():
        dirs = start.shape[0]
        for t in range(0, acts.shape[0], size):
            at = slice(t, t + size)
            proj[size:, at] = nt(start[size:, :], acts[at, :]).astype(BF16)
        cover(size, dirs)

    cover(0, size)
    for copy in others:
        copy.wait()
    finish(hi, lo, *work, in_ref, op_ref, moved_ref, out_any, fb, sem, rest)


def image_kernel(image_any, in_any, op_any, moved_ref, out_any, fb, part, hi, lo, *rest):
    *work, in_ref, op_ref, sems, sem = rest
    copies = [
        pltpu.make_async_copy(in_any, in_ref, sems.at[0]),
        pltpu.make_async_copy(op_any, op_ref, sems.at[1]),
    ]
    for copy in copies:
        copy.start()

    def taken(i):
        c = pltpu.make_async_copy(image_any.at[:, tile(i, part.shape[1])], part, sems.at[2])
        c.start()
        c.wait()
        high, low = split(part[...])
        hi[:, tile(i, part.shape[1])] = high
        lo[:, tile(i, part.shape[1])] = low

    loop(hi.shape[1] // part.shape[1], taken)
    for copy in copies:
        copy.wait()
    finish(hi, lo, *work, in_ref, op_ref, moved_ref, out_any, fb, sem, lambda: None)


def work_scratch(dirs, width, in_shape, op_shape):
    square = pltpu.VMEM((dirs, dirs), BF16)
    return [
        pltpu.VMEM((dirs, width), BF16),
        pltpu.VMEM((dirs, width), BF16),
        pltpu.VMEM((dirs, dirs), F32),
        square,
        square,
        pltpu.VMEM((4 * B, dirs), BF16),
        square,
        square,
        pltpu.VMEM((2 * B, width), BF16),
        pltpu.VMEM((2 * B, width), BF16),
        pltpu.VMEM((2, dirs, B), F32),
        pltpu.VMEM((dirs, B), F32),
        pltpu.VMEM((B, B), F32),
        pltpu.VMEM((dirs // B, B, B), F32),
        pltpu.VMEM((dirs // (2 * B) - 1, op_shape[0], 2 * B), BF16),
        pltpu.VMEM(in_shape, BF16),
        pltpu.VMEM(op_shape, BF16),
    ]


def ring_items(own, perms, count, cut):
    forward, backward = perms
    behind, ahead = [own], [own]
    for _ in range((count - 1) // 2):
        behind.append(lax.ppermute(behind[-1], "group", forward))
        ahead.append(lax.ppermute(ahead[-1], "group", backward))
    last = [
        lax.ppermute(behind[-1][:cut], "group", forward),
        lax.ppermute(ahead[-1][cut:], "group", backward),
    ]
    return behind + ahead[1:] + last


def per_device(acts, start_basis, out_proj, in_proj):
    tokens, width = acts[0], acts.shape[2]
    dirs = start_basis.shape[2]
    count = lax.axis_size("group")
    in_next = passed_along(in_proj[0], "section", -1)
    out_shape = (
        jax.ShapeDtypeStruct((dirs, in_next.shape[1]), BF16),
        jax.ShapeDtypeStruct((out_proj.shape[1], dirs), BF16),
        jax.ShapeDtypeStruct((2 * B, width), BF16),
    )
    scratch = work_scratch(dirs, width, in_next.shape, out_proj[0].shape)
    leaving = pltpu.SemaphoreType.DMA((dirs // (2 * B) - 1,))
    n_tokens = count * tokens.shape[0]
    hbm, vmem = pl.BlockSpec(memory_space=pl.ANY), pl.BlockSpec(memory_space=pltpu.VMEM)
    params = pltpu.CompilerParams(vmem_limit_bytes=VMEM_BYTES)
    if count % 2 == 0 and n_tokens * width * 2 <= GATHER_LIMIT and (width // count) % B == 0:
        order = list(range(0, count, 2)) + list(range(count - 1, 0, -2))
        forward = [(order[i], order[(i + 1) % count]) for i in range(count)]
        perms = (forward, [(b, a) for a, b in forward])
        s_items = ring_items(start_basis[0].T.astype(BF16), perms, count, dirs // 2)
        a_items = ring_items(tokens, perms, count, tokens.shape[0] // 2)
        gathered = [pltpu.VMEM((n_tokens, width), BF16), pltpu.VMEM((dirs, width), BF16)]
        sems = pltpu.SemaphoreType.DMA((2 * len(a_items) + 2,))
        moved, rotated, final = pl.pallas_call(
            functools.partial(gathered_kernel, count),
            out_shape=out_shape,
            in_specs=[hbm] * (2 * len(a_items) + 2),
            out_specs=(vmem, hbm, vmem),
            scratch_shapes=[*gathered, pltpu.VMEM((dirs, n_tokens), BF16), *scratch, sems, leaving],
            compiler_params=params,
        )(*a_items, *s_items, in_next, out_proj[0])
    else:
        lowered = lax.all_gather(start_basis[0].astype(BF16), "group", axis=0, tiled=True)
        projected = jnp.dot(tokens, lowered, preferred_element_type=F32).astype(BF16)
        partial = lax.dot_general(
            tokens, projected, (((0,), (0,)), ((), ())), preferred_element_type=F32
        )
        part = lax.psum_scatter(partial, "group", scatter_dimension=0, tiled=True)
        image = lax.all_gather(part, "group", axis=0, tiled=True)
        moved, rotated, final = pl.pallas_call(
            image_kernel,
            out_shape=out_shape,
            in_specs=[hbm] * 3,
            out_specs=(vmem, hbm, vmem),
            scratch_shapes=[
                pltpu.VMEM((dirs, 256), F32),
                *scratch,
                pltpu.SemaphoreType.DMA((3,)),
                leaving,
            ],
            compiler_params=params,
        )(image.T, in_next, out_proj[0])
    rotated_in = passed_along(moved, "section", 1)
    pieces = 4 if out_proj.shape[1] % 256 == 0 else 1
    rotated_out = pl.pallas_call(
        functools.partial(last_kernel, pieces),
        out_shape=out_shape[1],
        in_specs=[vmem, hbm, hbm],
        out_specs=hbm,
        scratch_shapes=[
            pltpu.VMEM(out_proj[0].shape, BF16),
            pltpu.VMEM((out_proj.shape[1], 2 * B), BF16),
            pltpu.SemaphoreType.DMA((2 * pieces,)),
        ],
        input_output_aliases={2: 0},
        compiler_params=pltpu.CompilerParams(vmem_limit_bytes=VMEM_BYTES),
        cost_estimate=pl.CostEstimate(
            flops=4 * B * width * out_proj.shape[1], bytes_accessed=6 << 20, transcendentals=0
        ),
    )(final, out_proj[0], rotated)
    return (rotated_out[None], rotated_in[None])


def solution(mesh):
    in_specs = (
        P("section", "group", None),
        P("section", "group", None),
        P("section", "group", None),
        P("section", None, "group"),
    )
    out_specs = (P("section", "group", None), P("section", None, "group"))
    return jax.shard_map(
        per_device, mesh=mesh, in_specs=in_specs, out_specs=out_specs, check_vma=False
    )
```

```python
import functools

import jax
import jax.numpy as jnp
from jax import lax
from jax.experimental import pallas as pl
from jax.experimental.pallas import tpu as pltpu
from jax.sharding import PartitionSpec as P

B = 128
F32, BF16 = jnp.float32, jnp.bfloat16
HIGH = lax.Precision.HIGHEST
GATHER_LIMIT = 16 << 20
VMEM_BYTES = 58 << 20


def passed_along(value, axis, steps):
    count = lax.axis_size(axis)
    pairs = [(source, (source + steps) % count) for source in range(count)]
    return lax.ppermute(value, axis, pairs)


def nn(a, b, **kw):
    return lax.dot_general(a, b, (((1,), (0,)), ((), ())), preferred_element_type=F32, **kw)


def nt(a, b, **kw):
    return lax.dot_general(a, b, (((1,), (1,)), ((), ())), preferred_element_type=F32, **kw)


def lane_of(x, j):
    return jnp.take_along_axis(x, jnp.full((8, B), j, jnp.int32), axis=1)


def row_of(x, s):
    return jnp.broadcast_to(x[s : s + 1, :], (8, B))


def factor_core(V):
    n = len(V)
    sub = lax.broadcasted_iota(jnp.int32, (8, B), 0)
    lane = lax.broadcasted_iota(jnp.int32, (8, B), 1)
    out = []
    for p in range(n):
        in_panel = (lane >= 8 * p) & (lane < 8 * p + 8)
        C = [lane_of(V[p], 8 * p + j) for j in range(8)]
        below = {i: [lane_of(V[i], 8 * p + j) for j in range(8)] for i in range(p + 1, n)}
        X = jnp.where(in_panel, (lane - 8 * p == sub).astype(F32), V[p])
        U = X
        pivots = jnp.ones((8, B), F32)
        d = row_of(C[0], 0)
        for j in range(8):
            inv = 1.0 / d
            pivots = jnp.where(sub == j, d, pivots)
            own, pivot_column = sub == j, C[j]
            if j < 7:
                d = row_of(C[j + 1], j + 1) - (row_of(C[j], j + 1) * row_of(C[j + 1], j)) * inv
            for k in range(j + 1, 8):
                s = row_of(C[k], j) * inv
                C[k] = jnp.where(own, s, C[k] - pivot_column * s)
            x = row_of(X, j) * inv
            X = jnp.where(own, x, X - pivot_column * x)
            if j < 7:
                U = U - jnp.where(sub > j, pivot_column * inv, 0.0) * row_of(U, j)
        row = sub + 8 * p
        out.append(jnp.where(lane <= row, U * lax.rsqrt(pivots), 0.0))
        for i in range(p + 1, n):
            t = [below[i][j] * row_of(X, j) for j in range(8)]
            V[i] = jnp.where(in_panel, 0.0, V[i]) - (
                ((t[0] + t[1]) + (t[2] + t[3])) + ((t[4] + t[5]) + (t[6] + t[7]))
            )
    return out


def split(x):
    hi = x.astype(BF16)
    return hi, (x - hi.astype(F32)).astype(BF16)


def loop(count, body):
    lax.fori_loop(0, count, lambda i, c: (body(i), c)[1], 0)


def tile(i, size):
    start = i * size
    return pl.ds(start if isinstance(start, int) else pl.multiple_of(start, size), size)


def three(dot, a, b):
    return dot(a[0], b[0]) + dot(a[0], b[1]) + dot(a[1], b[0])


def factor_block(diag, w):
    for i, row in enumerate(factor_core([diag[8 * i : 8 * i + 8, :] for i in range(B // 8)])):
        w[8 * i : 8 * i + 8, :] = row


def stacked(pair, high, low):
    size = pair.shape[0] // 2
    both = nn(pair, high)
    return both[:size] + both[size:] + nn(pair[:size], low)


def finish(hi, lo, gram, lhi, llo, ecat, whi, wlo, yhi, ylo, cols, base, diag, wd, outs, in_ref, op_ref, moved_ref, out_any, fb, sem, rest):
    dirs, width = hi.shape
    n, size = dirs // B, 2 * B
    lanes = range(0, width, size)

    def gram_part(r, end, c):
        a, b = hi[c : c + size, :], lo[c : c + size, :]
        x, y = hi[r:end, :], lo[r:end, :]
        gram[r:end, c : c + size] = nt(x, a) + nt(x, b) + nt(y, a)

    def first_columns(r, end):
        gram_part(r, end, 0)
        cols[0, r:end, :] = gram[r:end, :B]
        base[r:end, :] = gram[r:end, B:size]

    first_columns(0, size)
    for ref in (whi, wlo):
        ref[...] = jnp.zeros(ref.shape, ref.dtype)
    diag[...] = gram[:B, :B]

    def prepare(c):
        m = c * size
        mine = slice(m, m + size)
        if m:
            left = lhi[mine, :m], llo[mine, :m]
            high, rest = split(three(nn, left, (whi[:m, :m], wlo[:m, :m])))
            ecat[:size, :m] = high
            ecat[size:, :m] = rest
        for d in lanes:
            at = slice(d, d + size)
            if m:
                y = hi[mine, at].astype(F32) + lo[mine, at].astype(F32)
                y = y - stacked(ecat[:, :m], hi[:m, at], lo[:m, at])
                yhi[:, at], ylo[:, at] = split(y)
            else:
                yhi[:, at], ylo[:, at] = hi[mine, at], lo[mine, at]

    def results(c):
        m = c * size
        mine = slice(m, m + size)
        first, second = slice(m, m + B), slice(m + B, m + size)
        wa, wb = split(wd[2 * c]), split(wd[2 * c + 1])
        between = three(nn, (lhi[second, first], llo[second, first]), wa)
        wab = -three(nn, wb, split(between))
        top = jnp.concatenate([wd[2 * c], jnp.zeros((B, B), F32)], axis=1)
        inv = split(jnp.concatenate([top, jnp.concatenate([wab, wd[2 * c + 1]], axis=1)], axis=0))
        pair = jnp.concatenate(inv, axis=0)
        more = m + size < dirs
        if more:
            whi[mine, mine], wlo[mine, mine] = inv
            if m:
                below = -three(nn, inv, (ecat[:size, :m], ecat[size:, :m]))
                whi[mine, :m], wlo[mine, :m] = split(below)
        for d in lanes:
            at = slice(d, d + size)
            fb[:, at] = stacked(pair, yhi[:, at], ylo[:, at]).astype(BF16)
        moved_ref[mine, :] = nn(fb[...], in_ref[...]).astype(BF16)
        if more:
            half = op_ref.shape[0] // 2
            for r in (0, half):
                outs[c, r : r + half, :] = nt(op_ref[r : r + half, :], fb[...]).astype(BF16)

    def update(k, first, end):
        r, then = k * B, 1 - k % 2
        pair = split(three(nt, split(cols[then, first:end, :]), split(wd[k - 1])))
        lhi[first:end, r - B : r], llo[first:end, r - B : r] = pair
        mine = lhi[r : r + B, r - B : r], llo[r : r + B, r - B : r]
        cols[k % 2, first:end, :] = base[first:end, :] - three(nt, pair, mine)

    def next_base(k):
        r, q = k * B, (k + 1) * B
        taken = (lhi[q:, :r], llo[q:, :r]), (lhi[q : q + B, :r], llo[q : q + B, :r])
        base[q:, :] = gram[q:, q : q + B] - three(nt, *taken)

    def block(k, beside):
        q = (k + 1) * B
        if k == 1:
            update(k, B, size)
        elif k:
            update(k, k * B, dirs)
            if q < dirs:
                next_base(k)
        beside()
        factor_block(diag, wd.at[k])
        if q < dirs:
            part = split(three(nt, split(cols[k % 2, q : q + B, :]), split(wd[k])))
            diag[...] = base[q : q + B, :] - three(nt, part, part)

    def late():
        if size < dirs:
            first_columns(size, dirs)
            update(1, size, dirs)
            gram_part(size, dirs, size)
            next_base(1)
        prepare(0)

    block(0, rest)
    block(1, late)
    def third():
        results(0)
        for c in range(2 * size, dirs, size):
            gram_part(c, dirs, c)

    for b in range(1, n // 2):
        block(2 * b, third if b == 1 else lambda: results(b - 1))
        block(2 * b + 1, lambda: prepare(b))
    leaving = [
        pltpu.make_async_copy(outs.at[c], out_any.at[:, pl.ds(c * size, size)], sem.at[c])
        for c in range(n // 2 - 1)
    ]
    for copy in leaving:
        copy.start()
    results(n // 2 - 1)
    for copy in leaving:
        copy.wait()


def last_kernel(pieces, fb, op_any, _, out_any, op, out, sems):
    rows, width = op.shape[0] // pieces, out.shape[1]
    at = pl.ds(out_any.shape[1] - width, width)
    each = [pl.ds(i * rows, rows) for i in range(pieces)]
    come = [pltpu.make_async_copy(op_any.at[r, :], op.at[r, :], sems.at[i]) for i, r in enumerate(each)]
    go = [
        pltpu.make_async_copy(out.at[r, :], out_any.at[r, at], sems.at[pieces + i])
        for i, r in enumerate(each)
    ]
    for copy in come:
        copy.start()
    for i in range(pieces):
        come[i].wait()
        out[each[i], :] = nt(op[each[i], :], fb[...]).astype(BF16)
        go[i].start()
    for copy in go:
        copy.wait()


def item_copies(count, a_items, s_items, acts, start, sems):
    full = (count - 1) // 2
    dirs, width = start.shape
    rows, cols = a_items[0].shape[0], width // count
    me = lax.axis_index("group")
    pos = jnp.where(me % 2 == 0, me // 2, count - 1 - me // 2)
    a_copies, s_copies, later = [], [], []
    for n in range(len(s_items)):
        if n < 2 * full + 1:
            step, slot, half, parts = (-n if n <= full else n - full), n, 0, 1
        else:
            step, slot, half, parts = count // 2, count - 1, n - (2 * full + 1), 2
        at = lax.rem(pos + step + count, count)
        owner = jnp.where(at < count // 2, 2 * at, 2 * (count - 1 - at) + 1)
        lanes = pl.ds(pl.multiple_of(owner * cols, cols), cols)
        if n < len(a_items):
            size = rows // parts
            to = acts.at[pl.ds(slot * rows + half * size, size), :]
            a_copies.append(pltpu.make_async_copy(a_items[n], to, sems.at[2 * n]))
        size = dirs // parts
        for r, end, into in ((0, 2 * B, s_copies), (2 * B, dirs, later)):
            r, end = max(r, half * size), min(end, half * size + size)
            if r < end:
                source = s_items[n].at[pl.ds(r - half * size, end - r), :]
                sem = sems.at[2 * len(s_items) + n if into is later else 2 * n + 1]
                into.append(pltpu.make_async_copy(source, start.at[pl.ds(r, end - r), lanes], sem))
    return a_copies, s_copies, later


def gathered_kernel(count, *refs):
    n_items = 2 * ((count - 1) // 2) + 3
    a_items, s_items = refs[:n_items], refs[n_items : 2 * n_items]
    in_any, op_any, moved_ref, out_any, fb = refs[2 * n_items : 2 * n_items + 5]
    acts, start, proj, hi, lo, *work, in_ref, op_ref, sems, sem = refs[2 * n_items + 5 :]
    a_copies, s_copies, later = item_copies(count, a_items, s_items, acts, start, sems)
    others = [
        *later,
        pltpu.make_async_copy(in_any, in_ref, sems.at[3 * n_items]),
        pltpu.make_async_copy(op_any, op_ref, sems.at[3 * n_items + 1]),
    ]
    for copy in s_copies + a_copies + others:
        copy.start()
    for copy in s_copies:
        copy.wait()
    rows, size = a_items[0].shape[0], 2 * B
    for n in range(0, count, 2):
        for copy in a_copies[n : n + 2] if n + 2 < count else a_copies[n:]:
            copy.wait()
        at = slice(n * rows, (n + 2) * rows)
        proj[:size, at] = nt(start[:size, :], acts[at, :]).astype(BF16)

    def cover(r, end):
        for d in range(0, hi.shape[1], size):
            at = slice(d, d + size)
            hi[r:end, at], lo[r:end, at] = split(nn(proj[r:end, :], acts[:, at]))

    def rest():
        dirs = start.shape[0]
        for t in range(0, acts.shape[0], size):
            at = slice(t, t + size)
            proj[size:, at] = nt(start[size:, :], acts[at, :]).astype(BF16)
        cover(size, dirs)

    cover(0, size)
    for copy in others:
        copy.wait()
    finish(hi, lo, *work, in_ref, op_ref, moved_ref, out_any, fb, sem, rest)


def image_kernel(image_any, in_any, op_any, moved_ref, out_any, fb, part, hi, lo, *rest):
    *work, in_ref, op_ref, sems, sem = rest
    copies = [
        pltpu.make_async_copy(in_any, in_ref, sems.at[0]),
        pltpu.make_async_copy(op_any, op_ref, sems.at[1]),
    ]
    for copy in copies:
        copy.start()

    def taken(i):
        c = pltpu.make_async_copy(image_any.at[:, tile(i, part.shape[1])], part, sems.at[2])
        c.start()
        c.wait()
        high, low = split(part[...])
        hi[:, tile(i, part.shape[1])] = high
        lo[:, tile(i, part.shape[1])] = low

    loop(hi.shape[1] // part.shape[1], taken)
    for copy in copies:
        copy.wait()
    finish(hi, lo, *work, in_ref, op_ref, moved_ref, out_any, fb, sem, lambda: None)


def work_scratch(dirs, width, in_shape, op_shape):
    square = pltpu.VMEM((dirs, dirs), BF16)
    return [
        pltpu.VMEM((dirs, width), BF16),
        pltpu.VMEM((dirs, width), BF16),
        pltpu.VMEM((dirs, dirs), F32),
        square,
        square,
        pltpu.VMEM((4 * B, dirs), BF16),
        square,
        square,
        pltpu.VMEM((2 * B, width), BF16),
        pltpu.VMEM((2 * B, width), BF16),
        pltpu.VMEM((2, dirs, B), F32),
        pltpu.VMEM((dirs, B), F32),
        pltpu.VMEM((B, B), F32),
        pltpu.VMEM((dirs // B, B, B), F32),
        pltpu.VMEM((dirs // (2 * B) - 1, op_shape[0], 2 * B), BF16),
        pltpu.VMEM(in_shape, BF16),
        pltpu.VMEM(op_shape, BF16),
    ]


def ring_items(own, perms, count, cut):
    forward, backward = perms
    behind, ahead = [own], [own]
    for _ in range((count - 1) // 2):
        behind.append(lax.ppermute(behind[-1], "group", forward))
        ahead.append(lax.ppermute(ahead[-1], "group", backward))
    last = [
        lax.ppermute(behind[-1][:cut], "group", forward),
        lax.ppermute(ahead[-1][cut:], "group", backward),
    ]
    return behind + ahead[1:] + last


def per_device(acts, start_basis, out_proj, in_proj):
    tokens, width = acts[0], acts.shape[2]
    dirs = start_basis.shape[2]
    count = lax.axis_size("group")
    in_next = passed_along(in_proj[0], "section", -1)
    out_shape = (
        jax.ShapeDtypeStruct((dirs, in_next.shape[1]), BF16),
        jax.ShapeDtypeStruct((out_proj.shape[1], dirs), BF16),
        jax.ShapeDtypeStruct((2 * B, width), BF16),
    )
    scratch = work_scratch(dirs, width, in_next.shape, out_proj[0].shape)
    leaving = pltpu.SemaphoreType.DMA((dirs // (2 * B) - 1,))
    n_tokens = count * tokens.shape[0]
    hbm, vmem = pl.BlockSpec(memory_space=pl.ANY), pl.BlockSpec(memory_space=pltpu.VMEM)
    params = pltpu.CompilerParams(vmem_limit_bytes=VMEM_BYTES)
    if count % 2 == 0 and n_tokens * width * 2 <= GATHER_LIMIT and (width // count) % B == 0:
        order = list(range(0, count, 2)) + list(range(count - 1, 0, -2))
        forward = [(order[i], order[(i + 1) % count]) for i in range(count)]
        perms = (forward, [(b, a) for a, b in forward])
        s_items = ring_items(start_basis[0].T.astype(BF16), perms, count, dirs // 2)
        a_items = ring_items(tokens, perms, count, tokens.shape[0] // 2)
        gathered = [pltpu.VMEM((n_tokens, width), BF16), pltpu.VMEM((dirs, width), BF16)]
        sems = pltpu.SemaphoreType.DMA((3 * len(a_items) + 2,))
        moved, rotated, final = pl.pallas_call(
            functools.partial(gathered_kernel, count),
            out_shape=out_shape,
            in_specs=[hbm] * (2 * len(a_items) + 2),
            out_specs=(vmem, hbm, vmem),
            scratch_shapes=[*gathered, pltpu.VMEM((dirs, n_tokens), BF16), *scratch, sems, leaving],
            compiler_params=params,
        )(*a_items, *s_items, in_next, out_proj[0])
    else:
        lowered = lax.all_gather(start_basis[0].astype(BF16), "group", axis=0, tiled=True)
        projected = jnp.dot(tokens, lowered, preferred_element_type=F32).astype(BF16)
        partial = lax.dot_general(
            tokens, projected, (((0,), (0,)), ((), ())), preferred_element_type=F32
        )
        part = lax.psum_scatter(partial, "group", scatter_dimension=0, tiled=True)
        image = lax.all_gather(part, "group", axis=0, tiled=True)
        moved, rotated, final = pl.pallas_call(
            image_kernel,
            out_shape=out_shape,
            in_specs=[hbm] * 3,
            out_specs=(vmem, hbm, vmem),
            scratch_shapes=[
                pltpu.VMEM((dirs, 256), F32),
                *scratch,
                pltpu.SemaphoreType.DMA((3,)),
                leaving,
            ],
            compiler_params=params,
        )(image.T, in_next, out_proj[0])
    rotated_in = passed_along(moved, "section", 1)
    pieces = 4 if out_proj.shape[1] % 256 == 0 else 1
    rotated_out = pl.pallas_call(
        functools.partial(last_kernel, pieces),
        out_shape=out_shape[1],
        in_specs=[vmem, hbm, hbm],
        out_specs=hbm,
        scratch_shapes=[
            pltpu.VMEM(out_proj[0].shape, BF16),
            pltpu.VMEM((out_proj.shape[1], 2 * B), BF16),
            pltpu.SemaphoreType.DMA((2 * pieces,)),
        ],
        input_output_aliases={2: 0},
        compiler_params=pltpu.CompilerParams(vmem_limit_bytes=VMEM_BYTES),
        cost_estimate=pl.CostEstimate(
            flops=4 * B * width * out_proj.shape[1], bytes_accessed=6 << 20, transcendentals=0
        ),
    )(final, out_proj[0], rotated)
    return (rotated_out[None], rotated_in[None])


def solution(mesh):
    in_specs = (
        P("section", "group", None),
        P("section", "group", None),
        P("section", "group", None),
        P("section", None, "group"),
    )
    out_specs = (P("section", "group", None), P("section", None, "group"))
    return jax.shard_map(
        per_device, mesh=mesh, in_specs=in_specs, out_specs=out_specs, check_vma=False
    )
```
